512 devices in a mesh: ctx: 64 (over z, y_hi, core), chan: 8 (over x, y_lo).
Axes of the slice: x: 4, y: 4 (y_hi: 2, y_lo: 2; y = y_hi * 2 + y_lo), z: 16, core: 2. Of those that a mesh axis runs over, the one named last changes fastest.
Arguments:
- sequence: bfloat16 [8192, 4096], P('ctx', 'chan'), may hold values from -6 to 6
- in_weight: bfloat16 [3, 4096, 2048], P(None, 'ctx', 'chan'), may hold values from -0.09375 to 0.09375
- short_taps: float32 [3, 7, 2048], P(None, None, 'chan'), may hold values from -2 to 2
- decay_rates: float32 [128, 16], P('chan'), may hold values from 3.0517578e-05 to 0.03
- residues: float32 [128, 16], P('chan'), may hold values from -1.5 to 1.5
- skip_gain: float32 [2048], P('chan'), may hold values from -5 to 5
Outputs:
- mixed: bfloat16 [8192, 2048], P('ctx', 'chan')
The draws below stay inside these ranges and needn't reach their ends.
All inputs are finite; a program needn't handle non-finite values.
Results may differ from the reference program's by a relative error of at most 0.0064.
Values may be sent and summed in bfloat16 or wider, within the bound.
No kernel may reach another device: no remote copies, remote signals or barrier semaphores. Data moves between devices by JAX's collectives and lax.ppermute only.
A program may use at most 64 MiB of HBM per device.

```python
import math
import jax
import jax.numpy as jnp
from jax import lax

D = 4096
CHANNELS = 2048
FGROUP = 16
ORDER = 16
TAPS = 7
TOKENS = 8192
FFTLEN = 16384
FILTERS = 128


def block_levels(own_key, shape, cuts, low, high):
    gain = 1.0
    for axis_at, blocks in cuts:
        steps = jax.random.uniform(jax.random.fold_in(jax.random.fold_in(own_key, 6), axis_at), (blocks,), jnp.float32, low / len(cuts), high / len(cuts))
        gain = gain * jnp.repeat(jnp.exp(steps), shape[axis_at] // blocks).reshape((-1,) + (1,) * (len(shape) - 1 - axis_at))
    return gain


def noise(stream_key, extent, scale, most, shards=(), kind=jnp.bfloat16):
    array = scale * jax.random.normal(stream_key, extent, jnp.float32)
    if shards:
        array = array * block_levels(stream_key, extent, shards, -0.22, 0.18)
    return jnp.clip(array, -most, most).astype(kind)


def setup_inputs(seed: int = 0) -> dict:
    streams_of = jax.random.split(jax.random.key(seed), 7)
    sequence = noise(streams_of[0], (TOKENS, D), 1.0, 6.0, ((0, 64), (1, 8)))
    in_weight = noise(streams_of[1], (3, D, CHANNELS), D ** -0.5, 0.09375, ((1, 64), (2, 8)))
    short_taps = noise(streams_of[2], (3, TAPS, CHANNELS), TAPS ** -0.5, 2.0, ((2, 8),), jnp.float32)
    decay_rates = jnp.clip(jnp.exp(math.log(0.03) - 6.89065 * jax.random.uniform(streams_of[3], (FILTERS, ORDER), jnp.float32) ** block_levels(streams_of[3], (FILTERS, ORDER), ((0, 8),), -0.2, 0.2)), 3.0517578125e-05, 0.03)
    residues = noise(streams_of[4], (FILTERS, ORDER), 0.25, 1.5, ((0, 8),), jnp.float32)
    skip_gain = noise(streams_of[5], (CHANNELS,), 1.0, 5.0, ((0, 8),), jnp.float32)
    return {"sequence": sequence, "in_weight": in_weight, "short_taps": short_taps, "decay_rates": decay_rates, "residues": residues, "skip_gain": skip_gain}


def reference(sequence, in_weight, short_taps, decay_rates, residues, skip_gain):
    projections = jnp.stack([jnp.dot(sequence, in_weight[slot], preferred_element_type=jnp.float32) for slot in range(3)]).astype(jnp.bfloat16)
    padded = jnp.pad(projections, ((0, 0), (TAPS - 1, 0), (0, 0)))
    filtered = jnp.zeros((3, TOKENS, CHANNELS), jnp.float32)
    for tap in range(TAPS):
        window = padded[:, TAPS - 1 - tap:TAPS - 1 - tap + TOKENS, :].astype(jnp.float32)
        filtered = filtered + short_taps[:, tap, None, :] * window
    query = filtered[0]
    signal = filtered[1] * filtered[2]
    moments = jnp.arange(TOKENS, dtype=jnp.float32)
    weights = residues * jnp.sqrt(2.0 * decay_rates)
    impulse = jnp.zeros((FILTERS, TOKENS), jnp.float32)
    for mode in range(ORDER):
        impulse = impulse + weights[:, mode, None] * jnp.exp(-decay_rates[:, mode, None] * moments[None, :])
    blocks = jnp.transpose(signal.reshape(TOKENS, FILTERS, FGROUP), (1, 0, 2))

    def convolve(pair):
        block, kernel = pair
        spectrum = jnp.fft.rfft(block, n=FFTLEN, axis=0) * jnp.fft.rfft(kernel, n=FFTLEN)[:, None]
        return jnp.fft.irfft(spectrum, n=FFTLEN, axis=0)[:TOKENS]
    conv = lax.map(convolve, (blocks, impulse))
    conv = jnp.transpose(conv, (1, 0, 2)).reshape(TOKENS, CHANNELS)
    return (query * (conv + skip_gain * signal)).astype(jnp.bfloat16)
```

```python
import functools

import jax
import jax.numpy as jnp
from jax import lax
from jax.experimental import pallas as pl
from jax.experimental.pallas import tpu as pltpu
from jax.sharding import Mesh
from jax.sharding import PartitionSpec as P

AXES = ("zh", "z0", "yh", "core", "x", "yl")
SIZES = (8, 2, 2, 2, 4, 2)
CTX = ("zh", "z0", "yh", "core")
CHAN = ("x", "yl")
RING = 8

ROWS = 128
HALO = 16
SPAN = 256
LANES = 128
GROUPS = 8
FGROUP = 16
ORDER = 16
TAPS = 7
COLS = 3 * LANES
DEPTH = 256
BLOCKS = 32
HIGHEST = lax.Precision.HIGHEST
F32 = jnp.float32
BF16 = jnp.bfloat16


def iota(shape, axis):
    return lax.broadcasted_iota(jnp.int32, shape, axis)


def exact_dot(a, b, dims):
    return lax.dot_general(a, b, (dims, ((), ())), precision=HIGHEST, preferred_element_type=F32)


def filter_kernel(rates_ref, residues_ref, high_ref, low_ref, reach_ref, decay_ref):
    half = lax.axis_index("z0")
    first = pl.multiple_of(half * GROUPS, GROUPS)
    rates = rates_ref[pl.ds(first, GROUPS), :]
    weights = residues_ref[pl.ds(first, GROUPS), :] * jnp.sqrt(2.0 * rates)
    slot = iota((GROUPS, SPAN), 1)
    lag = jnp.where(slot == 0, 0, SPAN - slot).astype(F32)
    impulse = jnp.zeros((GROUPS, SPAN), F32)
    for mode in range(ORDER):
        impulse = impulse + weights[:, mode : mode + 1] * jnp.exp(
            -rates[:, mode : mode + 1] * lag
        )
    causal = iota((SPAN, SPAN), 0) >= iota((SPAN, SPAN), 1)
    left = (SPAN - 1 - iota((ORDER, SPAN), 1)).astype(F32)
    for group in range(GROUPS):
        columns = slice(group * SPAN, (group + 1) * SPAN)
        spread = jnp.broadcast_to(impulse[group : group + 1, :], (SPAN, SPAN))
        rolled = pltpu.roll(spread, 0, 1, stride=1, stride_axis=0)
        toeplitz = jnp.where(causal, rolled, 0.0)
        high = toeplitz.astype(BF16)
        high_ref[0:SPAN, columns] = high
        low_ref[0:SPAN, columns] = (toeplitz - high.astype(F32)).astype(BF16)
        pick = (iota((GROUPS, SPAN), 0) == group).astype(F32)
        state = jnp.exp(-exact_dot(rates, pick, ((0,), (0,))) * left)
        high = state.astype(BF16)
        high_ref[SPAN : SPAN + ORDER, columns] = high
        low_ref[SPAN : SPAN + ORDER, columns] = (state - high.astype(F32)).astype(BF16)
    mode_pick = (iota((ORDER, LANES), 0) == iota((ORDER, LANES), 1) % ORDER).astype(F32)
    own = iota((GROUPS, LANES), 0) == iota((GROUPS, LANES), 1) // ORDER
    flat_rates = jnp.sum(
        jnp.where(own, exact_dot(rates, mode_pick, ((1,), (0,))), 0.0), axis=0, keepdims=True
    )
    flat_weights = jnp.sum(
        jnp.where(own, exact_dot(weights, mode_pick, ((1,), (0,))), 0.0), axis=0, keepdims=True
    )
    ahead = (iota((SPAN, LANES), 0) + 1).astype(F32)
    reach_ref[...] = flat_weights * jnp.exp(-flat_rates * ahead)
    decay_ref[...] = jnp.exp(-float(SPAN) * exact_dot(rates, own.astype(F32), ((0,), (0,))))


def matmul_kernel(*refs):
    x_ref, blocks = refs[0], refs[1 : 1 + RING]
    keep_ref, send_ref = refs[1 + RING :]
    core = lax.axis_index("core")
    here = lax.axis_index("zh")
    for out_ref, group in ((keep_ref, core), (send_ref, 1 - core)):
        first = jnp.zeros((HALO + ROWS, COLS), F32)
        second = jnp.zeros((ROWS, COLS), F32)
        for step in range(RING):
            source = lax.rem(here + RING - step, RING)
            weight = blocks[step][...]
            first = first + jnp.dot(
                x_ref[group, 0, source], weight, preferred_element_type=F32
            )
            second = second + jnp.dot(
                x_ref[group, 1, source, HALO:, :], weight, preferred_element_type=F32
            )
        out_ref[0 : HALO + ROWS, :] = first
        out_ref[HALO + ROWS :, :] = second


def scan_kernel(
    keep_ref, recv_ref, taps_ref, high_ref, low_ref, query_ref, signal_ref, local_ref, state_ref, rows_ref
):
    half = lax.axis_index("z0")
    lanes = pl.ds(pl.multiple_of(half * LANES, LANES), LANES)
    total = keep_ref[...] + recv_ref[...]
    rows_ref[...] = total.astype(BF16).astype(F32)

    filtered = []
    for part in range(3):
        columns = slice(part * LANES, (part + 1) * LANES)
        value = jnp.zeros((SPAN, LANES), F32)
        for tap in range(TAPS):
            value = value + taps_ref[part, tap : tap + 1, lanes] * rows_ref[
                HALO - tap : HALO - tap + SPAN, columns
            ]
        filtered.append(value)
    query_ref[...] = filtered[0]
    signal = filtered[1] * filtered[2]
    signal_ref[...] = signal
    high = signal.astype(BF16)
    low = (signal - high.astype(F32)).astype(BF16)
    owner = iota((SPAN, LANES), 1) // FGROUP
    acc = jnp.zeros((SPAN + ORDER, LANES), F32)
    for group in range(GROUPS):
        columns = slice(group * SPAN, (group + 1) * SPAN)
        mine = owner == group
        high_part = jnp.where(mine, high, jnp.zeros_like(high))
        low_part = jnp.where(mine, low, jnp.zeros_like(low))
        acc = acc + jnp.dot(high_ref[:, columns], high_part, preferred_element_type=F32)
        acc = acc + jnp.dot(high_ref[:, columns], low_part, preferred_element_type=F32)
        acc = acc + jnp.dot(low_ref[:, columns], high_part, preferred_element_type=F32)
    local_ref[...] = acc[0:SPAN]
    state_ref[...] = jnp.broadcast_to(acc[SPAN:][None], (BLOCKS, ORDER, LANES))


def output_kernel(states_ref, decay_ref, reach_ref, query_ref, signal_ref, local_ref, gain_ref, out_ref):
    half = lax.axis_index("z0")
    lanes = pl.ds(pl.multiple_of(half * LANES, LANES), LANES)
    place = 4 * lax.axis_index("zh") + 2 * lax.axis_index("core") + lax.axis_index("yh")
    decay = decay_ref[...]
    carry = jnp.zeros((ORDER, LANES), F32)
    for block in range(BLOCKS - 1):
        outer, core, yh = block // 4, block // 2 % 2, block % 2
        state = states_ref[outer * 4 + yh * 2 + core]
        carry = jnp.where(block < place, carry * decay + state, carry)
    tiled = jnp.concatenate([carry] * GROUPS, axis=0)
    shape = (GROUPS * ORDER, LANES)
    tiled = jnp.where(iota(shape, 0) // ORDER == iota(shape, 1) // FGROUP, tiled, 0.0)
    conv = local_ref[...] + exact_dot(reach_ref[...], tiled, ((1,), (0,)))
    mixed = query_ref[...] * (conv + gain_ref[0:1, lanes] * signal_ref[...])
    mixed = mixed.astype(BF16)
    for side in range(2):
        for part in range(2):
            out_ref[side, part] = mixed[part * ROWS : (part + 1) * ROWS]


def call(kernel, shapes, *operands, scratch=()):
    return pl.pallas_call(
        kernel,
        out_shape=[jax.ShapeDtypeStruct(shape, dtype) for shape, dtype in shapes],
        in_specs=[pl.BlockSpec(memory_space=pltpu.VMEM)] * len(operands),
        out_specs=[pl.BlockSpec(memory_space=pltpu.VMEM)] * len(shapes),
        scratch_shapes=list(scratch),
    )(*operands)


def ring_shift(block, distance):
    return lax.ppermute(block, "zh", [(i, (i + distance) % RING) for i in range(RING)])


def per_device(sequence, in_weight, short_taps, decay_rates, residues, skip_gain):
    halves = in_weight.reshape(3, 64, 2, LANES).transpose(2, 1, 0, 3).reshape(2, 1, 64, COLS)
    slots = jnp.broadcast_to(halves, (2, 2, 64, COLS)).reshape(4, 64, COLS)
    block = lax.all_to_all(slots, ("z0", "yh"), 0, 0, tiled=True).reshape(DEPTH, COLS)
    blocks = [None] * RING
    blocks[0] = block
    up, down = block, block
    for step in range(1, RING // 2 + 1):
        up = ring_shift(up, 1)
        blocks[step] = up
        if step < RING // 2:
            down = ring_shift(down, -1)
            blocks[RING - step] = down
    count = 64
    edge = lax.ppermute(sequence[ROWS - HALO :], CTX, [(i, i + 1) for i in range(count - 1)])
    rows = jnp.concatenate([edge, sequence], axis=0)
    halves = rows.reshape(HALO + ROWS, 4, 2, 64).transpose(2, 0, 1, 3)
    halves = halves.reshape(1, 2, 1, HALO + ROWS, DEPTH)
    slots = jnp.broadcast_to(halves, (2, 2, RING, HALO + ROWS, DEPTH))
    slots = slots.reshape(4 * RING, HALO + ROWS, DEPTH)
    whole = lax.all_to_all(slots, ("z0", "core") + CHAN, 0, 0, tiled=True)
    whole = whole.reshape(2, 2, RING, HALO + ROWS, DEPTH)

    high, low, reach, decay = call(
        filter_kernel,
        [
            ((SPAN + ORDER, GROUPS * SPAN), BF16),
            ((SPAN + ORDER, GROUPS * SPAN), BF16),
            ((SPAN, LANES), F32),
            ((ORDER, LANES), F32),
        ],
        decay_rates,
        residues,
    )
    keep, send = call(
        matmul_kernel, [((HALO + SPAN, COLS), F32)] * 2, whole, *blocks
    )
    recv = lax.ppermute(send, "core", [(0, 1), (1, 0)])
    query, signal, local, states = call(
        scan_kernel,
        [((SPAN, LANES), F32)] * 3 + [((BLOCKS, ORDER, LANES), F32)],
        keep,
        recv,
        short_taps,
        high,
        low,
        scratch=[pltpu.VMEM((HALO + SPAN, COLS), F32)],
    )
    states = lax.all_to_all(states, ("zh", "yh", "core"), 0, 0, tiled=True)
    (slots,) = call(
        output_kernel,
        [((2, 2, ROWS, LANES), BF16)],
        states,
        decay,
        reach,
        query,
        signal,
        local,
        skip_gain[None],
    )
    slots = lax.all_to_all(slots.reshape(4, ROWS, LANES), ("z0", "core"), 0, 0, tiled=True)
    slots = slots.reshape(2, 2, ROWS, LANES)
    own = lax.dynamic_index_in_dim(slots, lax.axis_index("z0"), 1, keepdims=False)
    return own.transpose(1, 0, 2).reshape(ROWS, 2 * LANES)


def solution(mesh):
    fine = Mesh(mesh.devices.reshape(SIZES), AXES)
    return jax.shard_map(
        per_device,
        mesh=fine,
        in_specs=(
            P(CTX, CHAN),
            P(None, CTX, CHAN),
            P(None, None, CHAN),
            P(CHAN, None),
            P(CHAN, None),
            P(CHAN),
        ),
        out_specs=P(CTX, CHAN),
        check_vma=False,
    )
```

```python
import functools

import jax
import jax.numpy as jnp
from jax import lax
from jax.experimental import pallas as pl
from jax.experimental.pallas import tpu as pltpu
from jax.sharding import Mesh
from jax.sharding import PartitionSpec as P

AXES = ("zh", "z0", "yh", "core", "x", "yl")
SIZES = (8, 2, 2, 2, 4, 2)
CTX = ("zh", "z0", "yh", "core")
CHAN = ("x", "yl")
RING = 8

ROWS = 128
HALO = 16
SPAN = 256
LANES = 128
SIDE = 64
GROUPS = 4
FGROUP = 16
ORDER = 16
TAPS = 7
COLS = 3 * LANES
DEPTH = 256
PEERS = 16
HIGHEST = lax.Precision.HIGHEST
F32 = jnp.float32
BF16 = jnp.bfloat16


def iota(shape, axis):
    return lax.broadcasted_iota(jnp.int32, shape, axis)


def exact_dot(a, b, dims):
    return lax.dot_general(a, b, (dims, ((), ())), precision=HIGHEST, preferred_element_type=F32)


def side_by_side(even, odd, core):
    low = iota(even.shape, 1) < SIDE
    lower = jnp.where(low, even, pltpu.roll(odd, SIDE, 1))
    upper = jnp.where(low, pltpu.roll(even, SIDE, 1), odd)
    return jnp.where(core == 0, lower, upper), jnp.where(core == 0, upper, lower)


def own_filters(ref, half, core):
    rows = ref[pl.ds(pl.multiple_of(half * 2 * GROUPS, 2 * GROUPS), 2 * GROUPS), :]
    return jnp.where(core == 0, rows[0:GROUPS], rows[GROUPS:])


def filter_kernel(rates_ref, residues_ref, high_ref, low_ref, reach_ref, decay_ref):
    half, core = lax.axis_index("z0"), lax.axis_index("core")
    rates = own_filters(rates_ref, half, core)
    weights = own_filters(residues_ref, half, core) * jnp.sqrt(2.0 * rates)
    slot = iota((GROUPS, SPAN), 1)
    lag = jnp.where(slot == 0, 0, SPAN - slot).astype(F32)
    impulse = jnp.zeros((GROUPS, SPAN), F32)
    for mode in range(ORDER):
        impulse = impulse + weights[:, mode : mode + 1] * jnp.exp(
            -rates[:, mode : mode + 1] * lag
        )
    causal = iota((SPAN, SPAN), 0) >= iota((SPAN, SPAN), 1)
    left = (SPAN - 1 - iota((ORDER, SPAN), 1)).astype(F32)
    for group in range(GROUPS):
        columns = slice(group * SPAN, (group + 1) * SPAN)
        spread = jnp.broadcast_to(impulse[group : group + 1, :], (SPAN, SPAN))
        rolled = pltpu.roll(spread, 0, 1, stride=1, stride_axis=0)
        toeplitz = jnp.where(causal, rolled, 0.0)
        high = toeplitz.astype(BF16)
        high_ref[0:SPAN, columns] = high
        low_ref[0:SPAN, columns] = (toeplitz - high.astype(F32)).astype(BF16)
        pick = (iota((GROUPS, SPAN), 0) == group).astype(F32)
        state = jnp.exp(-exact_dot(rates, pick, ((0,), (0,))) * left)
        high = state.astype(BF16)
        high_ref[SPAN : SPAN + ORDER, columns] = high
        low_ref[SPAN : SPAN + ORDER, columns] = (state - high.astype(F32)).astype(BF16)
    shape = (GROUPS, GROUPS * ORDER)
    mode_pick = iota((ORDER, shape[1]), 0) == iota((ORDER, shape[1]), 1) % ORDER
    own = iota(shape, 0) == iota(shape, 1) // ORDER

    def flat(values):
        wide = exact_dot(values, mode_pick.astype(F32), ((1,), (0,)))
        return jnp.sum(jnp.where(own, wide, 0.0), axis=0, keepdims=True)

    ahead = (iota((SPAN, shape[1]), 0) + 1).astype(F32)
    reach_ref[...] = flat(weights) * jnp.exp(-flat(rates) * ahead)
    lanes = iota((GROUPS, LANES), 1) % SIDE // FGROUP == iota((GROUPS, LANES), 0)
    decay_ref[...] = jnp.exp(-float(SPAN) * exact_dot(rates, lanes.astype(F32), ((0,), (0,))))


def matmul_kernel(*refs):
    x_ref, blocks = refs[0], refs[1 : 1 + RING]
    keep_ref, send_ref, sums_ref = refs[1 + RING :]
    core = lax.axis_index("core")
    here = lax.axis_index("zh")
    for group in range(2):
        first = jnp.zeros((HALO + ROWS, COLS), F32)
        second = jnp.zeros((ROWS, COLS), F32)
        for step in range(RING):
            source = lax.rem(here + RING - step, RING)
            weight = blocks[step][...]
            first = first + jnp.dot(
                x_ref[source, group, 0], weight, preferred_element_type=F32
            )
            second = second + jnp.dot(
                x_ref[source, group, 1, HALO:, :], weight, preferred_element_type=F32
            )
        sums_ref[group, 0 : HALO + ROWS, :] = first
        sums_ref[group, HALO + ROWS :, :] = second
    for part in range(3):
        columns = slice(part * LANES, (part + 1) * LANES)
        keep_ref[:, columns], send_ref[:, columns] = side_by_side(
            sums_ref[0, :, columns], sums_ref[1, :, columns], core
        )


def scan_kernel(
    keep_ref, recv_ref, taps_ref, high_ref, low_ref, query_ref, signal_ref, local_ref, state_ref, rows_ref
):
    half, core = lax.axis_index("z0"), lax.axis_index("core")
    lanes = pl.ds(pl.multiple_of(half * LANES, LANES), LANES)
    total = keep_ref[...] + recv_ref[...]
    rows_ref[...] = total.astype(BF16).astype(F32)
    filtered = []
    for part in range(3):
        columns = slice(part * LANES, (part + 1) * LANES)
        taps = taps_ref[part, :, lanes]
        taps, _ = side_by_side(taps, taps, core)
        value = jnp.zeros((SPAN, LANES), F32)
        for tap in range(TAPS):
            value = value + taps[tap : tap + 1, :] * rows_ref[
                HALO - tap : HALO - tap + SPAN, columns
            ]
        filtered.append(value)
    query_ref[...] = filtered[0]
    signal = filtered[1] * filtered[2]
    signal_ref[...] = signal
    high = signal.astype(BF16)
    low = (signal - high.astype(F32)).astype(BF16)
    owner = iota((SPAN, LANES), 1) % SIDE // FGROUP
    acc = jnp.zeros((SPAN + ORDER, LANES), F32)
    for group in range(GROUPS):
        columns = slice(group * SPAN, (group + 1) * SPAN)
        mine = owner == group
        high_part = jnp.where(mine, high, jnp.zeros_like(high))
        low_part = jnp.where(mine, low, jnp.zeros_like(low))
        acc = acc + jnp.dot(high_ref[:, columns], high_part, preferred_element_type=F32)
        acc = acc + jnp.dot(high_ref[:, columns], low_part, preferred_element_type=F32)
        acc = acc + jnp.dot(low_ref[:, columns], high_part, preferred_element_type=F32)
    local_ref[...] = acc[0:SPAN]
    state_ref[...] = jnp.broadcast_to(acc[SPAN:][None], (PEERS, ORDER, LANES))


def output_kernel(states_ref, decay_ref, reach_ref, query_ref, signal_ref, local_ref, gain_ref, out_ref):
    half, core = lax.axis_index("z0"), lax.axis_index("core")
    lanes = pl.ds(pl.multiple_of(half * LANES, LANES), LANES)
    low = iota((ORDER, LANES), 1) < SIDE
    place = 4 * lax.axis_index("zh") + lax.axis_index("yh") + jnp.where(low, 0, 2)
    decay = decay_ref[...]
    carry = jnp.zeros((ORDER, LANES), F32)
    for block in range(2 * PEERS - 1):
        outer, odd, yh = block // 4, block // 2 % 2, block % 2
        state = states_ref[outer * 2 + yh]
        other = pltpu.roll(state, SIDE, 1)
        state = jnp.where(low, other, state) if odd else jnp.where(low, state, other)
        carry = jnp.where(block < place, carry * decay + state, carry)
    tiled = jnp.concatenate([carry] * GROUPS, axis=0)
    shape = (GROUPS * ORDER, LANES)
    tiled = jnp.where(iota(shape, 0) // ORDER == iota(shape, 1) % SIDE // FGROUP, tiled, 0.0)
    conv = local_ref[...] + exact_dot(reach_ref[...], tiled, ((1,), (0,)))
    gain = jnp.broadcast_to(gain_ref[0:1, lanes], (8, LANES))
    gain, _ = side_by_side(gain, gain, core)
    mixed = query_ref[...] * (conv + gain[0:1] * signal_ref[...])
    for run, value in enumerate((mixed, pltpu.roll(mixed, SIDE, 1))):
        value = value[:, 0:SIDE].astype(BF16)
        for part in range(2):
            out_ref[run, part] = value[part * ROWS : (part + 1) * ROWS]


def call(kernel, shapes, *operands, scratch=(), limit=16):
    return pl.pallas_call(
        kernel,
        out_shape=[jax.ShapeDtypeStruct(shape, dtype) for shape, dtype in shapes],
        in_specs=[pl.BlockSpec(memory_space=pltpu.VMEM)] * len(operands),
        out_specs=[pl.BlockSpec(memory_space=pltpu.VMEM)] * len(shapes),
        scratch_shapes=list(scratch),
        compiler_params=pltpu.CompilerParams(vmem_limit_bytes=limit << 20),
    )(*operands)


def ring_shift(block, distance):
    return lax.ppermute(block, "zh", [(i, (i + distance) % RING) for i in range(RING)])


def per_device(sequence, in_weight, short_taps, decay_rates, residues, skip_gain):
    halves = in_weight.reshape(3, 64, 2, LANES).transpose(2, 1, 0, 3).reshape(2, 1, 64, COLS)
    slots = jnp.broadcast_to(halves, (2, 2, 64, COLS)).reshape(4, 64, COLS)
    block = lax.all_to_all(slots, ("z0", "yh"), 0, 0, tiled=True).reshape(DEPTH, COLS)
    blocks = [None] * RING
    blocks[0] = block
    up, down = block, block
    for step in range(1, RING // 2 + 1):
        up = ring_shift(up, 1)
        blocks[step] = up
        if step < RING // 2:
            down = ring_shift(down, -1)
            blocks[RING - step] = down
    count = 64
    edge = lax.ppermute(sequence[ROWS - HALO :], CTX, [(i, i + 1) for i in range(count - 1)])
    rows = jnp.concatenate([edge, sequence], axis=0)
    halves = rows.reshape(HALO + ROWS, 4, 2, 64).transpose(2, 0, 1, 3)
    halves = halves.reshape(1, 2, HALO + ROWS, DEPTH)
    slots = jnp.broadcast_to(halves, (2, 2, HALO + ROWS, DEPTH))
    near = lax.all_to_all(
        slots.reshape(4, HALO + ROWS, DEPTH), ("z0", "core"), 0, 0, tiled=True
    )
    slots = jnp.broadcast_to(near[None], (RING, 4, HALO + ROWS, DEPTH))
    whole = lax.all_to_all(slots, CHAN, 0, 0, tiled=True)
    whole = whole.reshape(RING, 2, 2, HALO + ROWS, DEPTH)

    high, low, reach, decay = call(
        filter_kernel,
        [
            ((SPAN + ORDER, GROUPS * SPAN), BF16),
            ((SPAN + ORDER, GROUPS * SPAN), BF16),
            ((SPAN, GROUPS * ORDER), F32),
            ((ORDER, LANES), F32),
        ],
        decay_rates,
        residues,
    )
    keep, send = call(
        matmul_kernel,
        [((HALO + SPAN, COLS), F32)] * 2,
        whole,
        *blocks,
        scratch=[pltpu.VMEM((2, HALO + SPAN, COLS), F32)],
    )
    recv = lax.ppermute(send, "core", [(0, 1), (1, 0)])
    query, signal, local, states = call(
        scan_kernel,
        [((SPAN, LANES), F32)] * 3 + [((PEERS, ORDER, LANES), F32)],
        keep,
        recv,
        short_taps,
        high,
        low,
        scratch=[pltpu.VMEM((HALO + SPAN, COLS), F32)],
    )
    states = lax.all_to_all(states, ("zh", "yh"), 0, 0, tiled=True)
    (slots,) = call(
        output_kernel,
        [((2, 2, ROWS, SIDE), BF16)],
        states,
        decay,
        reach,
        query,
        signal,
        local,
        skip_gain[None],
    )
    slots = lax.all_to_all(slots.reshape(4, ROWS, SIDE), ("z0", "core"), 0, 0, tiled=True)
    return slots.transpose(1, 0, 2).reshape(ROWS, 4 * SIDE)


def solution(mesh):
    fine = Mesh(mesh.devices.reshape(SIZES), AXES)
    return jax.shard_map(
        per_device,
        mesh=fine,
        in_specs=(
            P(CTX, CHAN),
            P(None, CTX, CHAN),
            P(None, None, CHAN),
            P(CHAN, None),
            P(CHAN, None),
            P(CHAN),
        ),
        out_specs=P(CTX, CHAN),
        check_vma=False,
    )
```

```python
import jax
import jax.numpy as jnp
from jax import lax
from jax.experimental import pallas as pl
from jax.experimental.pallas import tpu as pltpu
from jax.sharding import Mesh
from jax.sharding import PartitionSpec as P


AXES = ("zh", "z0", "yh", "core", "x", "yl")
SIZES = (8, 2, 2, 2, 4, 2)
CTX = ("zh", "z0", "yh", "core")
CHAN = ("x", "yl")
RING = 8

ROWS = 128
HALO = 16
SPAN = 256
LANES = 128
SIDE = 64
GROUPS = 4
FGROUP = 16
ORDER = 16
TAPS = 7
COLS = 3 * LANES
DEPTH = 256
PEERS = 16
HIGHEST = lax.Precision.HIGHEST
F32 = jnp.float32
BF16 = jnp.bfloat16


def iota(shape, axis):
    return lax.broadcasted_iota(jnp.int32, shape, axis)


def exact_dot(a, b, dims):
    return lax.dot_general(a, b, (dims, ((), ())), precision=HIGHEST, preferred_element_type=F32)


def side_by_side(even, odd, core):
    low = iota(even.shape, 1) < SIDE
    lower = jnp.where(low, even, pltpu.roll(odd, SIDE, 1))
    upper = jnp.where(low, pltpu.roll(even, SIDE, 1), odd)
    return jnp.where(core == 0, lower, upper), jnp.where(core == 0, upper, lower)


def own_filters(ref, half, core):
    rows = ref[pl.ds(pl.multiple_of(half * 2 * GROUPS, 2 * GROUPS), 2 * GROUPS), :]
    return jnp.where(core == 0, rows[0:GROUPS], rows[GROUPS:])


def filter_kernel(rates_ref, residues_ref, high_ref, low_ref, reach_ref, decay_ref):
    half, core = lax.axis_index("z0"), lax.axis_index("core")
    rates = own_filters(rates_ref, half, core)
    weights = own_filters(residues_ref, half, core) * jnp.sqrt(2.0 * rates)
    slot = iota((GROUPS, SPAN), 1)
    lag = jnp.where(slot == 0, 0, SPAN - slot).astype(F32)
    impulse = jnp.zeros((GROUPS, SPAN), F32)
    for mode in range(ORDER):
        impulse = impulse + weights[:, mode : mode + 1] * jnp.exp(
            -rates[:, mode : mode + 1] * lag
        )
    causal = iota((SPAN, SPAN), 0) >= iota((SPAN, SPAN), 1)
    left = (SPAN - 1 - iota((ORDER, SPAN), 1)).astype(F32)
    for group in range(GROUPS):
        columns = slice(group * SPAN, (group + 1) * SPAN)
        spread = jnp.broadcast_to(impulse[group : group + 1, :], (SPAN, SPAN))
        rolled = pltpu.roll(spread, 0, 1, stride=1, stride_axis=0)
        toeplitz = jnp.where(causal, rolled, 0.0)
        high = toeplitz.astype(BF16)
        high_ref[0:SPAN, columns] = high
        low_ref[0:SPAN, columns] = (toeplitz - high.astype(F32)).astype(BF16)
        pick = (iota((GROUPS, SPAN), 0) == group).astype(F32)
        state = jnp.exp(-exact_dot(rates, pick, ((0,), (0,))) * left)
        high = state.astype(BF16)
        high_ref[SPAN : SPAN + ORDER, columns] = high
        low_ref[SPAN : SPAN + ORDER, columns] = (state - high.astype(F32)).astype(BF16)
    shape = (GROUPS, GROUPS * ORDER)
    mode_pick = iota((ORDER, shape[1]), 0) == iota((ORDER, shape[1]), 1) % ORDER
    own = iota(shape, 0) == iota(shape, 1) // ORDER

    def flat(values):
        wide = exact_dot(values, mode_pick.astype(F32), ((1,), (0,)))
        return jnp.sum(jnp.where(own, wide, 0.0), axis=0, keepdims=True)

    ahead = (iota((SPAN, shape[1]), 0) + 1).astype(F32)
    reach_ref[...] = flat(weights) * jnp.exp(-flat(rates) * ahead)
    lanes = iota((GROUPS, LANES), 1) % SIDE // FGROUP == iota((GROUPS, LANES), 0)
    decay_ref[...] = jnp.exp(-float(SPAN) * exact_dot(rates, lanes.astype(F32), ((0,), (0,))))


def matmul_kernel(*refs):
    x_ref, blocks = refs[0], refs[1 : 1 + RING]
    keep_ref, send_ref, sums_ref = refs[1 + RING :]
    core = lax.axis_index("core")
    here = lax.axis_index("zh")
    for group in range(2):
        first = jnp.zeros((HALO + ROWS, COLS), F32)
        second = jnp.zeros((ROWS, COLS), F32)
        for step in range(RING):
            source = lax.rem(here + RING - step, RING)
            weight = blocks[step][...]
            first = first + jnp.dot(
                x_ref[source, group, 0], weight, preferred_element_type=F32
            )
            second = second + jnp.dot(
                x_ref[source, group, 1, HALO:, :], weight, preferred_element_type=F32
            )
        sums_ref[group, 0 : HALO + ROWS, :] = first
        sums_ref[group, HALO + ROWS :, :] = second
    for part in range(3):
        columns = slice(part * LANES, (part + 1) * LANES)
        keep_ref[:, columns], send_ref[:, columns] = side_by_side(
            sums_ref[0, :, columns], sums_ref[1, :, columns], core
        )


def scan_kernel(
    keep_ref, recv_ref, taps_ref, high_ref, low_ref, query_ref, signal_ref, local_ref, state_ref, rows_ref
):
    half, core = lax.axis_index("z0"), lax.axis_index("core")
    lanes = pl.ds(pl.multiple_of(half * LANES, LANES), LANES)
    total = keep_ref[...] + recv_ref[...]
    rows_ref[...] = total.astype(BF16).astype(F32)
    filtered = []
    for part in range(3):
        columns = slice(part * LANES, (part + 1) * LANES)
        taps = taps_ref[part, :, lanes]
        taps, _ = side_by_side(taps, taps, core)
        value = jnp.zeros((SPAN, LANES), F32)
        for tap in range(TAPS):
            value = value + taps[tap : tap + 1, :] * rows_ref[
                HALO - tap : HALO - tap + SPAN, columns
            ]
        filtered.append(value)
    query_ref[...] = filtered[0]
    signal = filtered[1] * filtered[2]
    signal_ref[...] = signal
    high = signal.astype(BF16)
    low = (signal - high.astype(F32)).astype(BF16)
    owner = iota((SPAN, LANES), 1) % SIDE // FGROUP
    acc = jnp.zeros((SPAN + ORDER, LANES), F32)
    for group in range(GROUPS):
        columns = slice(group * SPAN, (group + 1) * SPAN)
        mine = owner == group
        high_part = jnp.where(mine, high, jnp.zeros_like(high))
        low_part = jnp.where(mine, low, jnp.zeros_like(low))
        acc = acc + jnp.dot(high_ref[:, columns], high_part, preferred_element_type=F32)
        acc = acc + jnp.dot(high_ref[:, columns], low_part, preferred_element_type=F32)
        acc = acc + jnp.dot(low_ref[:, columns], high_part, preferred_element_type=F32)
    local_ref[...] = acc[0:SPAN]
    state_ref[...] = jnp.broadcast_to(acc[SPAN:][None], (PEERS, ORDER, LANES))


def output_kernel(states_ref, decay_ref, reach_ref, query_ref, signal_ref, local_ref, gain_ref, out_ref):
    half, core = lax.axis_index("z0"), lax.axis_index("core")
    lanes = pl.ds(pl.multiple_of(half * LANES, LANES), LANES)
    low = iota((ORDER, LANES), 1) < SIDE
    place = 4 * lax.axis_index("zh") + lax.axis_index("yh") + jnp.where(low, 0, 2)
    decay = decay_ref[...]
    carry = jnp.zeros((ORDER, LANES), F32)
    for block in range(2 * PEERS - 1):
        outer, odd, yh = block // 4, block // 2 % 2, block % 2
        state = states_ref[outer * 2 + yh]
        other = pltpu.roll(state, SIDE, 1)
        state = jnp.where(low, other, state) if odd else jnp.where(low, state, other)
        carry = jnp.where(block < place, carry * decay + state, carry)
    tiled = jnp.concatenate([carry] * GROUPS, axis=0)
    shape = (GROUPS * ORDER, LANES)
    tiled = jnp.where(iota(shape, 0) // ORDER == iota(shape, 1) % SIDE // FGROUP, tiled, 0.0)
    conv = local_ref[...] + exact_dot(reach_ref[...], tiled, ((1,), (0,)))
    gain = jnp.broadcast_to(gain_ref[0:1, lanes], (8, LANES))
    gain, _ = side_by_side(gain, gain, core)
    mixed = query_ref[...] * (conv + gain[0:1] * signal_ref[...])
    for run, value in enumerate((mixed, pltpu.roll(mixed, SIDE, 1))):
        value = value[:, 0:SIDE].astype(BF16)
        for part in range(2):
            out_ref[run, part] = value[part * ROWS : (part + 1) * ROWS]


def call(kernel, shapes, *operands, scratch=(), limit=16):
    return pl.pallas_call(
        kernel,
        out_shape=[jax.ShapeDtypeStruct(shape, dtype) for shape, dtype in shapes],
        in_specs=[pl.BlockSpec(memory_space=pltpu.VMEM)] * len(operands),
        out_specs=[pl.BlockSpec(memory_space=pltpu.VMEM)] * len(shapes),
        scratch_shapes=list(scratch),
        compiler_params=pltpu.CompilerParams(vmem_limit_bytes=limit << 20),
    )(*operands)


def ring_shift(block, distance):
    return lax.ppermute(block, "zh", [(i, (i + distance) % RING) for i in range(RING)])


def per_device(sequence, in_weight, short_taps, decay_rates, residues, skip_gain):
    halves = [
        jnp.concatenate(
            [in_weight[part, :, side * LANES : (side + 1) * LANES] for part in range(3)], axis=1
        )
        for side in range(2)
    ]
    slots = jnp.stack([halves[0], halves[0], halves[1], halves[1]])
    block = lax.all_to_all(slots, ("z0", "yh"), 0, 0, tiled=True).reshape(DEPTH, COLS)
    blocks = [None] * RING
    blocks[0] = block
    up, down = block, block
    for step in range(1, RING // 2 + 1):
        up = ring_shift(up, 1)
        blocks[step] = up
        if step < RING // 2:
            down = ring_shift(down, -1)
            blocks[RING - step] = down
    count = 64
    edge = lax.ppermute(sequence[ROWS - HALO :], CTX, [(i, i + 1) for i in range(count - 1)])
    rows = jnp.concatenate([edge, sequence], axis=0)
    halves = rows.reshape(HALO + ROWS, 4, 2, 64).transpose(2, 0, 1, 3)
    halves = halves.reshape(1, 2, HALO + ROWS, DEPTH)
    slots = jnp.broadcast_to(halves, (2, 2, HALO + ROWS, DEPTH))
    near = lax.all_to_all(slots.reshape(4, HALO + ROWS, DEPTH), ("z0", "core"), 0, 0, tiled=True)
    slots = jnp.broadcast_to(near[None], (RING, 4, HALO + ROWS, DEPTH))
    whole = lax.all_to_all(slots, CHAN, 0, 0, tiled=True)
    whole = whole.reshape(RING, 2, 2, HALO + ROWS, DEPTH)

    high, low, reach, decay = call(
        filter_kernel,
        [
            ((SPAN + ORDER, GROUPS * SPAN), BF16),
            ((SPAN + ORDER, GROUPS * SPAN), BF16),
            ((SPAN, GROUPS * ORDER), F32),
            ((ORDER, LANES), F32),
        ],
        decay_rates,
        residues,
    )
    keep, send = call(
        matmul_kernel,
        [((HALO + SPAN, COLS), F32)] * 2,
        whole,
        *blocks,
        scratch=[pltpu.VMEM((2, HALO + SPAN, COLS), F32)],
    )
    recv = lax.ppermute(send, "core", [(0, 1), (1, 0)])
    query, signal, local, states = call(
        scan_kernel,
        [((SPAN, LANES), F32)] * 3 + [((PEERS, ORDER, LANES), F32)],
        keep,
        recv,
        short_taps,
        high,
        low,
        scratch=[pltpu.VMEM((HALO + SPAN, COLS), F32)],
    )
    states = lax.all_to_all(states, ("zh", "yh"), 0, 0, tiled=True)
    (slots,) = call(
        output_kernel,
        [((2, 2, ROWS, SIDE), BF16)],
        states,
        decay,
        reach,
        query,
        signal,
        local,
        skip_gain[None],
    )
    slots = lax.all_to_all(slots.reshape(4, ROWS, SIDE), ("z0", "core"), 0, 0, tiled=True)
    return slots.transpose(1, 0, 2).reshape(ROWS, 4 * SIDE)


def solution(mesh):
    fine = Mesh(mesh.devices.reshape(SIZES), AXES)
    return jax.shard_map(
        per_device,
        mesh=fine,
        in_specs=(
            P(CTX, CHAN),
            P(None, CTX, CHAN),
            P(None, None, CHAN),
            P(CHAN, None),
            P(CHAN, None),
            P(CHAN),
        ),
        out_specs=P(CTX, CHAN),
        check_vma=False,
    )
```

```python
import jax
import jax.numpy as jnp
from jax import lax
from jax.experimental import pallas as pl
from jax.experimental.pallas import tpu as pltpu
from jax.sharding import Mesh
from jax.sharding import PartitionSpec as P


AXES = ("zh", "z0", "yh", "core", "x", "yl")
SIZES = (8, 2, 2, 2, 4, 2)
CTX = ("zh", "z0", "yh", "core")
CHAN = ("x", "yl")
RING = 8

ROWS = 128
HALO = 16
SPAN = 256
LANES = 128
SIDE = 64
GROUPS = 4
FGROUP = 16
ORDER = 16
TAPS = 7
COLS = 3 * LANES
DEPTH = 256
PEERS = 16
HIGHEST = lax.Precision.HIGHEST
F32 = jnp.float32
BF16 = jnp.bfloat16


def iota(shape, axis):
    return lax.broadcasted_iota(jnp.int32, shape, axis)


def exact_dot(a, b, dims):
    return lax.dot_general(a, b, (dims, ((), ())), precision=HIGHEST, preferred_element_type=F32)


def side_by_side(even, odd, core):
    low = iota(even.shape, 1) < SIDE
    lower = jnp.where(low, even, pltpu.roll(odd, SIDE, 1))
    upper = jnp.where(low, pltpu.roll(even, SIDE, 1), odd)
    if isinstance(core, int):
        return (upper, lower) if core else (lower, upper)
    return jnp.where(core == 0, lower, upper), jnp.where(core == 0, upper, lower)


def own_filters(ref, half, core):
    rows = ref[pl.ds(pl.multiple_of(half * 2 * GROUPS, 2 * GROUPS), 2 * GROUPS), :]
    return jnp.where(core == 0, rows[0:GROUPS], rows[GROUPS:])


def filter_kernel(rates_ref, residues_ref, high_ref, low_ref, reach_ref, decay_ref):
    half, core = lax.axis_index("z0"), lax.axis_index("core")
    rates = own_filters(rates_ref, half, core)
    weights = own_filters(residues_ref, half, core) * jnp.sqrt(2.0 * rates)
    slot = iota((GROUPS, SPAN), 1)
    lag = jnp.where(slot == 0, 0, SPAN - slot).astype(F32)
    impulse = jnp.zeros((GROUPS, SPAN), F32)
    for mode in range(ORDER):
        impulse = impulse + weights[:, mode : mode + 1] * jnp.exp(
            -rates[:, mode : mode + 1] * lag
        )
    causal = iota((SPAN, SPAN), 0) >= iota((SPAN, SPAN), 1)
    left = (SPAN - 1 - iota((ORDER, SPAN), 1)).astype(F32)
    for group in range(GROUPS):
        columns = slice(group * SPAN, (group + 1) * SPAN)
        spread = jnp.broadcast_to(impulse[group : group + 1, :], (SPAN, SPAN))
        rolled = pltpu.roll(spread, 0, 1, stride=1, stride_axis=0)
        toeplitz = jnp.where(causal, rolled, 0.0)
        high = toeplitz.astype(BF16)
        high_ref[0:SPAN, columns] = high
        low_ref[0:SPAN, columns] = (toeplitz - high.astype(F32)).astype(BF16)
        pick = (iota((GROUPS, SPAN), 0) == group).astype(F32)
        state = jnp.exp(-exact_dot(rates, pick, ((0,), (0,))) * left)
        high = state.astype(BF16)
        high_ref[SPAN : SPAN + ORDER, columns] = high
        low_ref[SPAN : SPAN + ORDER, columns] = (state - high.astype(F32)).astype(BF16)
    shape = (GROUPS, GROUPS * ORDER)
    mode_pick = iota((ORDER, shape[1]), 0) == iota((ORDER, shape[1]), 1) % ORDER
    own = iota(shape, 0) == iota(shape, 1) // ORDER

    def flat(values):
        wide = exact_dot(values, mode_pick.astype(F32), ((1,), (0,)))
        return jnp.sum(jnp.where(own, wide, 0.0), axis=0, keepdims=True)

    ahead = (iota((SPAN, shape[1]), 0) + 1).astype(F32)
    reach_ref[...] = flat(weights) * jnp.exp(-flat(rates) * ahead)
    lanes = iota((GROUPS, LANES), 1) % SIDE // FGROUP == iota((GROUPS, LANES), 0)
    decay_ref[...] = jnp.exp(-float(SPAN) * exact_dot(rates, lanes.astype(F32), ((0,), (0,))))


def deal_kernel(rows_ref, out_ref, edge_ref):
    rows = rows_ref[...].astype(F32)
    for pair in range(DEPTH // LANES):
        first = 2 * pair * LANES
        even = rows[:, first : first + LANES]
        odd = rows[:, first + LANES : first + 2 * LANES]
        columns = slice(pair * LANES, (pair + 1) * LANES)
        for core, value in enumerate(side_by_side(even, odd, 0)):
            value = value.astype(BF16)
            out_ref[core, :, columns] = value
            edge_ref[core, :, columns] = value[ROWS - HALO :]


def near_kernel(edge_ref, dealt_ref, out_ref):
    for run in range(2):
        out_ref[run, :, 0:HALO, :] = edge_ref[...]
        out_ref[run, :, HALO:, :] = dealt_ref[...]


def fan_kernel(near_ref, out_ref):
    for run in range(2):
        first, second = near_ref[run, 0], near_ref[run, 1, HALO:, :]
        for target in range(RING):
            out_ref[target, run, 0 : HALO + ROWS, :] = first
            out_ref[target, run, HALO + ROWS :, :] = second


LAST = (RING // 2, RING // 2 + 1)
FIRST = tuple(step for step in range(RING) if step not in LAST)


def add_products(x_ref, blocks, steps, totals):
    here = lax.axis_index("zh")
    for step, block in zip(steps, blocks):
        source = lax.rem(here + RING - step, RING)
        rows = [
            jnp.concatenate([block[near, part] for part in range(3)], axis=1)
            for near in range(4)
        ]
        weight = jnp.concatenate(rows, axis=0)
        totals = [
            total + jnp.dot(x_ref[source, group], weight, preferred_element_type=F32)
            for group, total in enumerate(totals)
        ]
    return totals


def early_kernel(x_ref, *refs):
    totals = [jnp.zeros((HALO + SPAN, COLS), F32)] * 2
    refs[-1][0], refs[-1][1] = add_products(x_ref, refs[:-1], FIRST, totals)


def late_kernel(x_ref, sums_ref, *refs):
    blocks, (keep_ref, send_ref) = refs[: len(LAST)], refs[len(LAST) :]
    core = lax.axis_index("core")
    even, odd = add_products(x_ref, blocks, LAST, [sums_ref[0], sums_ref[1]])
    for part in range(3):
        columns = slice(part * LANES, (part + 1) * LANES)
        keep_ref[:, columns], send_ref[:, columns] = side_by_side(
            even[:, columns], odd[:, columns], core
        )


def scan_kernel(
    keep_ref, recv_ref, taps_ref, high_ref, low_ref, query_ref, signal_ref, local_ref, state_ref, rows_ref
):
    half, core = lax.axis_index("z0"), lax.axis_index("core")
    lanes = pl.ds(pl.multiple_of(half * LANES, LANES), LANES)
    total = keep_ref[...] + recv_ref[...]
    rows_ref[...] = total.astype(BF16).astype(F32)
    filtered = []
    for part in range(3):
        columns = slice(part * LANES, (part + 1) * LANES)
        taps = taps_ref[part, :, lanes]
        taps, _ = side_by_side(taps, taps, core)
        value = jnp.zeros((SPAN, LANES), F32)
        for tap in range(TAPS):
            value = value + taps[tap : tap + 1, :] * rows_ref[
                HALO - tap : HALO - tap + SPAN, columns
            ]
        filtered.append(value)
    query_ref[...] = filtered[0]
    signal = filtered[1] * filtered[2]
    signal_ref[...] = signal
    high = signal.astype(BF16)
    low = (signal - high.astype(F32)).astype(BF16)
    owner = iota((SPAN, LANES), 1) % SIDE // FGROUP
    acc = jnp.zeros((SPAN + ORDER, LANES), F32)
    for group in range(GROUPS):
        columns = slice(group * SPAN, (group + 1) * SPAN)
        mine = owner == group
        high_part = jnp.where(mine, high, jnp.zeros_like(high))
        low_part = jnp.where(mine, low, jnp.zeros_like(low))
        acc = acc + jnp.dot(high_ref[:, columns], high_part, preferred_element_type=F32)
        acc = acc + jnp.dot(high_ref[:, columns], low_part, preferred_element_type=F32)
        acc = acc + jnp.dot(low_ref[:, columns], high_part, preferred_element_type=F32)
    local_ref[...] = acc[0:SPAN]
    state_ref[...] = jnp.broadcast_to(acc[SPAN:][None], (PEERS, ORDER, LANES))


def output_kernel(states_ref, decay_ref, reach_ref, query_ref, signal_ref, local_ref, gain_ref, out_ref):
    half, core = lax.axis_index("z0"), lax.axis_index("core")
    lanes = pl.ds(pl.multiple_of(half * LANES, LANES), LANES)
    low = iota((ORDER, LANES), 1) < SIDE
    place = 4 * lax.axis_index("zh") + lax.axis_index("yh") + jnp.where(low, 0, 2)
    decay = decay_ref[...]
    carry = jnp.zeros((ORDER, LANES), F32)
    for block in range(2 * PEERS - 1):
        outer, odd, yh = block // 4, block // 2 % 2, block % 2
        state = states_ref[outer * 2 + yh]
        other = pltpu.roll(state, SIDE, 1)
        state = jnp.where(low, other, state) if odd else jnp.where(low, state, other)
        carry = jnp.where(block < place, carry * decay + state, carry)
    tiled = jnp.concatenate([carry] * GROUPS, axis=0)
    shape = (GROUPS * ORDER, LANES)
    tiled = jnp.where(iota(shape, 0) // ORDER == iota(shape, 1) % SIDE // FGROUP, tiled, 0.0)
    conv = local_ref[...] + exact_dot(reach_ref[...], tiled, ((1,), (0,)))
    gain = jnp.broadcast_to(gain_ref[0:1, lanes], (8, LANES))
    gain, _ = side_by_side(gain, gain, core)
    mixed = query_ref[...] * (conv + gain[0:1] * signal_ref[...])
    for run, value in enumerate((mixed, pltpu.roll(mixed, SIDE, 1))):
        value = value[:, 0:SIDE].astype(BF16)
        for part in range(2):
            out_ref[run, part] = value[part * ROWS : (part + 1) * ROWS]


def call(kernel, shapes, *operands, scratch=(), limit=16):
    return pl.pallas_call(
        kernel,
        out_shape=[jax.ShapeDtypeStruct(shape, dtype) for shape, dtype in shapes],
        in_specs=[pl.BlockSpec(memory_space=pltpu.VMEM)] * len(operands),
        out_specs=[pl.BlockSpec(memory_space=pltpu.VMEM)] * len(shapes),
        scratch_shapes=list(scratch),
        compiler_params=pltpu.CompilerParams(vmem_limit_bytes=limit << 20),
    )(*operands)


def ring_shift(block, distance):
    return lax.ppermute(block, "zh", [(i, (i + distance) % RING) for i in range(RING)])


def per_device(sequence, in_weight, short_taps, decay_rates, residues, skip_gain):
    halves = [in_weight[:, :, side * LANES : (side + 1) * LANES] for side in range(2)]
    slots = jnp.stack([halves[0], halves[0], halves[1], halves[1]])
    block = lax.all_to_all(slots, ("z0", "yh"), 0, 0, tiled=True)
    blocks = [None] * RING
    blocks[0] = block
    up, down = block, block
    for step in range(1, RING // 2 + 1):
        up = ring_shift(up, 1)
        blocks[step] = up
        if step < RING // 2:
            down = ring_shift(down, -1)
            blocks[RING - step] = down
    count = 64
    dealt, edge = call(deal_kernel, [((2, ROWS, DEPTH), BF16), ((2, HALO, DEPTH), BF16)], sequence)
    edge = lax.ppermute(edge, CTX, [(i, i + 1) for i in range(count - 1)])
    (slots,) = call(near_kernel, [((2, 2, HALO + ROWS, DEPTH), BF16)], edge, dealt)
    near = lax.all_to_all(slots.reshape(4, HALO + ROWS, DEPTH), ("z0", "core"), 0, 0, tiled=True)
    (slots,) = call(
        fan_kernel, [((RING, 2, HALO + SPAN, DEPTH), BF16)], near.reshape(2, 2, HALO + ROWS, DEPTH)
    )
    whole = lax.all_to_all(slots, CHAN, 0, 0, tiled=True)

    high, low, reach, decay = call(
        filter_kernel,
        [
            ((SPAN + ORDER, GROUPS * SPAN), BF16),
            ((SPAN + ORDER, GROUPS * SPAN), BF16),
            ((SPAN, GROUPS * ORDER), F32),
            ((ORDER, LANES), F32),
        ],
        decay_rates,
        residues,
    )
    (sums,) = call(
        early_kernel, [((2, HALO + SPAN, COLS), F32)], whole, *[blocks[step] for step in FIRST]
    )
    keep, send = call(
        late_kernel, [((HALO + SPAN, COLS), F32)] * 2, whole, sums, *[blocks[step] for step in LAST]
    )
    recv = lax.ppermute(send, "core", [(0, 1), (1, 0)])
    query, signal, local, states = call(
        scan_kernel,
        [((SPAN, LANES), F32)] * 3 + [((PEERS, ORDER, LANES), F32)],
        keep,
        recv,
        short_taps,
        high,
        low,
        scratch=[pltpu.VMEM((HALO + SPAN, COLS), F32)],
    )
    states = lax.all_to_all(states, ("zh", "yh"), 0, 0, tiled=True)
    (slots,) = call(
        output_kernel,
        [((2, 2, ROWS, SIDE), BF16)],
        states,
        decay,
        reach,
        query,
        signal,
        local,
        skip_gain[None],
    )
    slots = lax.all_to_all(slots.reshape(4, ROWS, SIDE), ("z0", "core"), 0, 0, tiled=True)
    return slots.transpose(1, 0, 2).reshape(ROWS, 4 * SIDE)


def solution(mesh):
    fine = Mesh(mesh.devices.reshape(SIZES), AXES)
    return jax.shard_map(
        per_device,
        mesh=fine,
        in_specs=(
            P(CTX, CHAN),
            P(None, CTX, CHAN),
            P(None, None, CHAN),
            P(CHAN, None),
            P(CHAN, None),
            P(CHAN),
        ),
        out_specs=P(CTX, CHAN),
        check_vma=False,
    )
```

```python
import jax
import jax.numpy as jnp
from jax import lax
from jax.experimental import pallas as pl
from jax.experimental.pallas import tpu as pltpu
from jax.sharding import Mesh
from jax.sharding import PartitionSpec as P


AXES = ("zh", "z0", "yh", "core", "x", "yl")
SIZES = (8, 2, 2, 2, 4, 2)
CTX = ("zh", "z0", "yh", "core")
CHAN = ("x", "yl")
RING = 8

ROWS = 128
HALO = 16
SPAN = 256
LANES = 128
SIDE = 64
GROUPS = 4
FGROUP = 16
ORDER = 16
TAPS = 7
COLS = 3 * LANES
DEPTH = 256
PEERS = 16
HIGHEST = lax.Precision.HIGHEST
F32 = jnp.float32
BF16 = jnp.bfloat16


def iota(shape, axis):
    return lax.broadcasted_iota(jnp.int32, shape, axis)


def exact_dot(a, b, dims):
    return lax.dot_general(a, b, (dims, ((), ())), precision=HIGHEST, preferred_element_type=F32)


def side_by_side(even, odd, core):
    low = iota(even.shape, 1) < SIDE
    lower = jnp.where(low, even, pltpu.roll(odd, SIDE, 1))
    upper = jnp.where(low, pltpu.roll(even, SIDE, 1), odd)
    if isinstance(core, int):
        return (upper, lower) if core else (lower, upper)
    return jnp.where(core == 0, lower, upper), jnp.where(core == 0, upper, lower)


def own_filters(ref, half, core):
    rows = ref[pl.ds(pl.multiple_of(half * 2 * GROUPS, 2 * GROUPS), 2 * GROUPS), :]
    return jnp.where(core == 0, rows[0:GROUPS], rows[GROUPS:])


def filter_kernel(rates_ref, residues_ref, high_ref, low_ref, reach_ref, decay_ref):
    half, core = lax.axis_index("z0"), lax.axis_index("core")
    rates = own_filters(rates_ref, half, core)
    weights = own_filters(residues_ref, half, core) * jnp.sqrt(2.0 * rates)
    slot = iota((GROUPS, SPAN), 1)
    lag = jnp.where(slot == 0, 0, SPAN - slot).astype(F32)
    impulse = jnp.zeros((GROUPS, SPAN), F32)
    for mode in range(ORDER):
        impulse = impulse + weights[:, mode : mode + 1] * jnp.exp(
            -rates[:, mode : mode + 1] * lag
        )
    causal = iota((SPAN, SPAN), 0) >= iota((SPAN, SPAN), 1)
    left = (SPAN - 1 - iota((ORDER, SPAN), 1)).astype(F32)
    for group in range(GROUPS):
        columns = slice(group * SPAN, (group + 1) * SPAN)
        spread = jnp.broadcast_to(impulse[group : group + 1, :], (SPAN, SPAN))
        rolled = pltpu.roll(spread, 0, 1, stride=1, stride_axis=0)
        toeplitz = jnp.where(causal, rolled, 0.0)
        high = toeplitz.astype(BF16)
        high_ref[0:SPAN, columns] = high
        low_ref[0:SPAN, columns] = (toeplitz - high.astype(F32)).astype(BF16)
        pick = (iota((GROUPS, SPAN), 0) == group).astype(F32)
        state = jnp.exp(-exact_dot(rates, pick, ((0,), (0,))) * left)
        high = state.astype(BF16)
        high_ref[SPAN : SPAN + ORDER, columns] = high
        low_ref[SPAN : SPAN + ORDER, columns] = (state - high.astype(F32)).astype(BF16)
    shape = (GROUPS, GROUPS * ORDER)
    mode_pick = iota((ORDER, shape[1]), 0) == iota((ORDER, shape[1]), 1) % ORDER
    own = iota(shape, 0) == iota(shape, 1) // ORDER

    def flat(values):
        wide = exact_dot(values, mode_pick.astype(F32), ((1,), (0,)))
        return jnp.sum(jnp.where(own, wide, 0.0), axis=0, keepdims=True)

    ahead = (iota((SPAN, shape[1]), 0) + 1).astype(F32)
    reach_ref[...] = flat(weights) * jnp.exp(-flat(rates) * ahead)
    lanes = iota((GROUPS, LANES), 1) % SIDE // FGROUP == iota((GROUPS, LANES), 0)
    decay_ref[...] = jnp.exp(-float(SPAN) * exact_dot(rates, lanes.astype(F32), ((0,), (0,))))


def deal_kernel(rows_ref, out_ref, edge_ref):
    rows = rows_ref[...].astype(F32)
    for pair in range(DEPTH // LANES):
        first = 2 * pair * LANES
        even = rows[:, first : first + LANES]
        odd = rows[:, first + LANES : first + 2 * LANES]
        columns = slice(pair * LANES, (pair + 1) * LANES)
        for core, value in enumerate(side_by_side(even, odd, 0)):
            value = value.astype(BF16)
            out_ref[core, :, columns] = value
            edge_ref[core, :, columns] = value[ROWS - HALO :]


def near_kernel(edge_ref, dealt_ref, out_ref):
    for run in range(2):
        out_ref[run, :, 0:HALO, :] = edge_ref[...]
        out_ref[run, :, HALO:, :] = dealt_ref[...]


def fan_kernel(near_ref, out_ref):
    for run in range(2):
        first, second = near_ref[run, 0], near_ref[run, 1, HALO:, :]
        for target in range(RING):
            out_ref[target, run, 0 : HALO + ROWS, :] = first
            out_ref[target, run, HALO + ROWS :, :] = second


SWAPS = ((0, 1, 7), (2, 6), (3, 5), (4,))


def add_products(x_ref, own, other, steps, totals):
    here = lax.axis_index("zh")
    for step, mine, theirs in zip(steps, own, other):
        source = lax.rem(here + RING - step, RING)
        rows = [
            jnp.concatenate([half[near, part] for part in range(3)], axis=1)
            for near in range(2)
            for half in (mine, theirs)
        ]
        weight = jnp.concatenate(rows, axis=0)
        totals = [
            total + jnp.dot(x_ref[source, group], weight, preferred_element_type=F32)
            for group, total in enumerate(totals)
        ]
    return totals


def block_refs(refs, groups):
    steps = [step for group in groups for step in group]
    own, stacks = refs[: len(steps)], refs[len(steps) : len(steps) + len(groups)]
    other = [
        stack.at[at] for stack, group in zip(stacks, groups) for at in range(len(group))
    ]
    return steps, own, other, refs[len(steps) + len(groups) :]


def for_each_yh(own, other, body):
    yh = lax.axis_index("yh")

    @pl.when(yh == 0)
    def _():
        body(own, other)

    @pl.when(yh == 1)
    def _():
        body(other, own)


def early_kernel(x_ref, *refs):
    steps, own, other, (out_ref,) = block_refs(refs, SWAPS[:2])

    def body(first, second):
        totals = [jnp.zeros((HALO + SPAN, COLS), F32)] * 2
        out_ref[0], out_ref[1] = add_products(x_ref, first, second, steps, totals)

    for_each_yh(own, other, body)


def late_kernel(x_ref, sums_ref, *refs):
    steps, own, other, (keep_ref, send_ref) = block_refs(refs, SWAPS[2:])
    core = lax.axis_index("core")

    def body(first, second):
        even, odd = add_products(x_ref, first, second, steps, [sums_ref[0], sums_ref[1]])
        for part in range(3):
            columns = slice(part * LANES, (part + 1) * LANES)
            keep_ref[:, columns], send_ref[:, columns] = side_by_side(
                even[:, columns], odd[:, columns], core
            )

    for_each_yh(own, other, body)


def scan_kernel(
    keep_ref, recv_ref, taps_ref, high_ref, low_ref, query_ref, signal_ref, local_ref, state_ref, rows_ref
):
    half, core = lax.axis_index("z0"), lax.axis_index("core")
    lanes = pl.ds(pl.multiple_of(half * LANES, LANES), LANES)
    total = keep_ref[...] + recv_ref[...]
    rows_ref[...] = total.astype(BF16).astype(F32)
    filtered = []
    for part in range(3):
        columns = slice(part * LANES, (part + 1) * LANES)
        taps = taps_ref[part, :, lanes]
        taps, _ = side_by_side(taps, taps, core)
        value = jnp.zeros((SPAN, LANES), F32)
        for tap in range(TAPS):
            value = value + taps[tap : tap + 1, :] * rows_ref[
                HALO - tap : HALO - tap + SPAN, columns
            ]
        filtered.append(value)
    query_ref[...] = filtered[0]
    signal = filtered[1] * filtered[2]
    signal_ref[...] = signal
    high = signal.astype(BF16)
    low = (signal - high.astype(F32)).astype(BF16)
    owner = iota((SPAN, LANES), 1) % SIDE // FGROUP
    acc = jnp.zeros((SPAN + ORDER, LANES), F32)
    for group in range(GROUPS):
        columns = slice(group * SPAN, (group + 1) * SPAN)
        mine = owner == group
        high_part = jnp.where(mine, high, jnp.zeros_like(high))
        low_part = jnp.where(mine, low, jnp.zeros_like(low))
        acc = acc + jnp.dot(high_ref[:, columns], high_part, preferred_element_type=F32)
        acc = acc + jnp.dot(high_ref[:, columns], low_part, preferred_element_type=F32)
        acc = acc + jnp.dot(low_ref[:, columns], high_part, preferred_element_type=F32)
    local_ref[...] = acc[0:SPAN]
    state_ref[...] = jnp.broadcast_to(acc[SPAN:][None], (PEERS, ORDER, LANES))


def output_kernel(states_ref, decay_ref, reach_ref, query_ref, signal_ref, local_ref, gain_ref, out_ref):
    half, core = lax.axis_index("z0"), lax.axis_index("core")
    lanes = pl.ds(pl.multiple_of(half * LANES, LANES), LANES)
    low = iota((ORDER, LANES), 1) < SIDE
    place = 4 * lax.axis_index("zh") + lax.axis_index("yh") + jnp.where(low, 0, 2)
    decay = decay_ref[...]
    carry = jnp.zeros((ORDER, LANES), F32)
    for block in range(2 * PEERS - 1):
        outer, odd, yh = block // 4, block // 2 % 2, block % 2
        state = states_ref[outer * 2 + yh]
        other = pltpu.roll(state, SIDE, 1)
        state = jnp.where(low, other, state) if odd else jnp.where(low, state, other)
        carry = jnp.where(block < place, carry * decay + state, carry)
    tiled = jnp.concatenate([carry] * GROUPS, axis=0)
    shape = (GROUPS * ORDER, LANES)
    tiled = jnp.where(iota(shape, 0) // ORDER == iota(shape, 1) % SIDE // FGROUP, tiled, 0.0)
    conv = local_ref[...] + exact_dot(reach_ref[...], tiled, ((1,), (0,)))
    gain = jnp.broadcast_to(gain_ref[0:1, lanes], (8, LANES))
    gain, _ = side_by_side(gain, gain, core)
    mixed = query_ref[...] * (conv + gain[0:1] * signal_ref[...])
    for run, value in enumerate((mixed, pltpu.roll(mixed, SIDE, 1))):
        value = value[:, 0:SIDE].astype(BF16)
        for part in range(2):
            out_ref[run, part] = value[part * ROWS : (part + 1) * ROWS]


def call(kernel, shapes, *operands, scratch=(), limit=16):
    return pl.pallas_call(
        kernel,
        out_shape=[jax.ShapeDtypeStruct(shape, dtype) for shape, dtype in shapes],
        in_specs=[pl.BlockSpec(memory_space=pltpu.VMEM)] * len(operands),
        out_specs=[pl.BlockSpec(memory_space=pltpu.VMEM)] * len(shapes),
        scratch_shapes=list(scratch),
        compiler_params=pltpu.CompilerParams(vmem_limit_bytes=limit << 20),
    )(*operands)


def ring_shift(block, distance):
    return lax.ppermute(block, "zh", [(i, (i + distance) % RING) for i in range(RING)])


def per_device(sequence, in_weight, short_taps, decay_rates, residues, skip_gain):
    slots = jnp.stack([in_weight[:, :, :LANES], in_weight[:, :, LANES:]])
    block = lax.all_to_all(slots, "z0", 0, 0, tiled=True)
    blocks = [None] * RING
    blocks[0] = block
    up, down = block, block
    for step in range(1, RING // 2 + 1):
        up = ring_shift(up, 1)
        blocks[step] = up
        if step < RING // 2:
            down = ring_shift(down, -1)
            blocks[RING - step] = down
    swapped = []
    for group in SWAPS:
        stack = jnp.stack([blocks[step] for step in group])
        swapped.append(lax.ppermute(stack, "yh", [(0, 1), (1, 0)]))
    count = 64
    dealt, edge = call(deal_kernel, [((2, ROWS, DEPTH), BF16), ((2, HALO, DEPTH), BF16)], sequence)
    edge = lax.ppermute(edge, CTX, [(i, i + 1) for i in range(count - 1)])
    (slots,) = call(near_kernel, [((2, 2, HALO + ROWS, DEPTH), BF16)], edge, dealt)
    near = lax.all_to_all(slots.reshape(4, HALO + ROWS, DEPTH), ("z0", "core"), 0, 0, tiled=True)
    (slots,) = call(
        fan_kernel, [((RING, 2, HALO + SPAN, DEPTH), BF16)], near.reshape(2, 2, HALO + ROWS, DEPTH)
    )
    whole = lax.all_to_all(slots, CHAN, 0, 0, tiled=True)

    high, low, reach, decay = call(
        filter_kernel,
        [
            ((SPAN + ORDER, GROUPS * SPAN), BF16),
            ((SPAN + ORDER, GROUPS * SPAN), BF16),
            ((SPAN, GROUPS * ORDER), F32),
            ((ORDER, LANES), F32),
        ],
        decay_rates,
        residues,
    )
    (sums,) = call(
        early_kernel,
        [((2, HALO + SPAN, COLS), F32)],
        whole,
        *[blocks[step] for group in SWAPS[:2] for step in group],
        *swapped[:2],
    )
    keep, send = call(
        late_kernel,
        [((HALO + SPAN, COLS), F32)] * 2,
        whole,
        sums,
        *[blocks[step] for group in SWAPS[2:] for step in group],
        *swapped[2:],
    )
    recv = lax.ppermute(send, "core", [(0, 1), (1, 0)])
    query, signal, local, states = call(
        scan_kernel,
        [((SPAN, LANES), F32)] * 3 + [((PEERS, ORDER, LANES), F32)],
        keep,
        recv,
        short_taps,
        high,
        low,
        scratch=[pltpu.VMEM((HALO + SPAN, COLS), F32)],
    )
    states = lax.all_to_all(states, ("zh", "yh"), 0, 0, tiled=True)
    (slots,) = call(
        output_kernel,
        [((2, 2, ROWS, SIDE), BF16)],
        states,
        decay,
        reach,
        query,
        signal,
        local,
        skip_gain[None],
    )
    slots = lax.all_to_all(slots.reshape(4, ROWS, SIDE), ("z0", "core"), 0, 0, tiled=True)
    return slots.transpose(1, 0, 2).reshape(ROWS, 4 * SIDE)


def solution(mesh):
    fine = Mesh(mesh.devices.reshape(SIZES), AXES)
    return jax.shard_map(
        per_device,
        mesh=fine,
        in_specs=(
            P(CTX, CHAN),
            P(None, CTX, CHAN),
            P(None, None, CHAN),
            P(CHAN, None),
            P(CHAN, None),
            P(CHAN),
        ),
        out_specs=P(CTX, CHAN),
        check_vma=False,
    )
```

```python
import jax
import jax.numpy as jnp
from jax import lax
from jax.experimental import pallas as pl
from jax.experimental.pallas import tpu as pltpu
from jax.sharding import Mesh
from jax.sharding import PartitionSpec as P


AXES = ("zh", "z0", "yh", "core", "x", "yl")
SIZES = (8, 2, 2, 2, 4, 2)
CTX = ("zh", "z0", "yh", "core")
CHAN = ("x", "yl")
RING = 8

ROWS = 128
HALO = 16
SPAN = 256
LANES = 128
SIDE = 64
GROUPS = 4
FGROUP = 16
ORDER = 16
TAPS = 7
COLS = 3 * LANES
DEPTH = 256
PEERS = 16
HIGHEST = lax.Precision.HIGHEST
F32 = jnp.float32
BF16 = jnp.bfloat16


def iota(shape, axis):
    return lax.broadcasted_iota(jnp.int32, shape, axis)


def exact_dot(a, b, dims):
    return lax.dot_general(a, b, (dims, ((), ())), precision=HIGHEST, preferred_element_type=F32)


def side_by_side(even, odd, core):
    low = iota(even.shape, 1) < SIDE
    lower = jnp.where(low, even, pltpu.roll(odd, SIDE, 1))
    upper = jnp.where(low, pltpu.roll(even, SIDE, 1), odd)
    if isinstance(core, int):
        return (upper, lower) if core else (lower, upper)
    return jnp.where(core == 0, lower, upper), jnp.where(core == 0, upper, lower)


def own_filters(ref, half, core):
    rows = ref[pl.ds(pl.multiple_of(half * 2 * GROUPS, 2 * GROUPS), 2 * GROUPS), :]
    return jnp.where(core == 0, rows[0:GROUPS], rows[GROUPS:])


def filter_kernel(rates_ref, residues_ref, high_ref, low_ref, reach_ref, decay_ref):
    half, core = lax.axis_index("z0"), lax.axis_index("core")
    rates = own_filters(rates_ref, half, core)
    weights = own_filters(residues_ref, half, core) * jnp.sqrt(2.0 * rates)
    slot = iota((GROUPS, SPAN), 1)
    lag = jnp.where(slot == 0, 0, SPAN - slot).astype(F32)
    impulse = jnp.zeros((GROUPS, SPAN), F32)
    for mode in range(ORDER):
        impulse = impulse + weights[:, mode : mode + 1] * jnp.exp(
            -rates[:, mode : mode + 1] * lag
        )
    causal = iota((SPAN, SPAN), 0) >= iota((SPAN, SPAN), 1)
    left = (SPAN - 1 - iota((ORDER, SPAN), 1)).astype(F32)
    for group in range(GROUPS):
        columns = slice(group * SPAN, (group + 1) * SPAN)
        spread = jnp.broadcast_to(impulse[group : group + 1, :], (SPAN, SPAN))
        rolled = pltpu.roll(spread, 0, 1, stride=1, stride_axis=0)
        toeplitz = jnp.where(causal, rolled, 0.0)
        high = toeplitz.astype(BF16)
        high_ref[0:SPAN, columns] = high
        low_ref[0:SPAN, columns] = (toeplitz - high.astype(F32)).astype(BF16)
        pick = (iota((GROUPS, SPAN), 0) == group).astype(F32)
        state = jnp.exp(-exact_dot(rates, pick, ((0,), (0,))) * left)
        high = state.astype(BF16)
        high_ref[SPAN : SPAN + ORDER, columns] = high
        low_ref[SPAN : SPAN + ORDER, columns] = (state - high.astype(F32)).astype(BF16)
    shape = (GROUPS, GROUPS * ORDER)
    mode_pick = iota((ORDER, shape[1]), 0) == iota((ORDER, shape[1]), 1) % ORDER
    own = iota(shape, 0) == iota(shape, 1) // ORDER

    def flat(values):
        wide = exact_dot(values, mode_pick.astype(F32), ((1,), (0,)))
        return jnp.sum(jnp.where(own, wide, 0.0), axis=0, keepdims=True)

    ahead = (iota((SPAN, shape[1]), 0) + 1).astype(F32)
    reach_ref[...] = flat(weights) * jnp.exp(-flat(rates) * ahead)
    lanes = iota((GROUPS, LANES), 1) % SIDE // FGROUP == iota((GROUPS, LANES), 0)
    decay_ref[...] = jnp.exp(-float(SPAN) * exact_dot(rates, lanes.astype(F32), ((0,), (0,))))


def deal_kernel(rows_ref, out_ref, edge_ref):
    rows = rows_ref[...].astype(F32)
    for pair in range(DEPTH // LANES):
        first = 2 * pair * LANES
        even = rows[:, first : first + LANES]
        odd = rows[:, first + LANES : first + 2 * LANES]
        columns = slice(pair * LANES, (pair + 1) * LANES)
        for core, value in enumerate(side_by_side(even, odd, 0)):
            value = value.astype(BF16)
            out_ref[core, :, columns] = value
            edge_ref[core, :, columns] = value[ROWS - HALO :]


def near_kernel(edge_ref, dealt_ref, out_ref):
    for run in range(2):
        out_ref[run, :, 0:HALO, :] = edge_ref[...]
        out_ref[run, :, HALO:, :] = dealt_ref[...]


def fan_kernel(near_ref, out_ref):
    for run in range(2):
        first, second = near_ref[run, 0], near_ref[run, 1, HALO:, :]
        for target in range(RING):
            out_ref[target, run, 0 : HALO + ROWS, :] = first
            out_ref[target, run, HALO + ROWS :, :] = second


LAST = (RING // 2, RING // 2 + 1)
FIRST = tuple(step for step in range(RING) if step not in LAST)


def add_products(x_ref, blocks, steps, totals):
    here = lax.axis_index("zh")
    for step, block in zip(steps, blocks):
        source = lax.rem(here + RING - step, RING)
        rows = [
            jnp.concatenate([block[near, part] for part in range(3)], axis=1)
            for near in range(4)
        ]
        weight = jnp.concatenate(rows, axis=0)
        totals = [
            total + jnp.dot(x_ref[source, group], weight, preferred_element_type=F32)
            for group, total in enumerate(totals)
        ]
    return totals


def early_kernel(x_ref, *refs):
    totals = [jnp.zeros((HALO + SPAN, COLS), F32)] * 2
    refs[-1][0], refs[-1][1] = add_products(x_ref, refs[:-1], FIRST, totals)


def late_kernel(x_ref, sums_ref, *refs):
    blocks, (keep_ref, send_ref) = refs[: len(LAST)], refs[len(LAST) :]
    core = lax.axis_index("core")
    even, odd = add_products(x_ref, blocks, LAST, [sums_ref[0], sums_ref[1]])
    for part in range(3):
        columns = slice(part * LANES, (part + 1) * LANES)
        keep_ref[:, columns], send_ref[:, columns] = side_by_side(
            even[:, columns], odd[:, columns], core
        )


def scan_kernel(
    keep_ref, recv_ref, taps_ref, high_ref, low_ref, query_ref, signal_ref, local_ref, state_ref, rows_ref
):
    half, core = lax.axis_index("z0"), lax.axis_index("core")
    lanes = pl.ds(pl.multiple_of(half * LANES, LANES), LANES)
    total = keep_ref[...] + recv_ref[...]
    rows_ref[...] = total.astype(BF16).astype(F32)
    filtered = []
    for part in range(3):
        columns = slice(part * LANES, (part + 1) * LANES)
        taps = taps_ref[part, :, lanes]
        taps, _ = side_by_side(taps, taps, core)
        value = jnp.zeros((SPAN, LANES), F32)
        for tap in range(TAPS):
            value = value + taps[tap : tap + 1, :] * rows_ref[
                HALO - tap : HALO - tap + SPAN, columns
            ]
        filtered.append(value)
    query_ref[...] = filtered[0]
    signal = filtered[1] * filtered[2]
    signal_ref[...] = signal
    high = signal.astype(BF16)
    low = (signal - high.astype(F32)).astype(BF16)
    owner = iota((SPAN, LANES), 1) % SIDE // FGROUP
    acc = jnp.zeros((SPAN + ORDER, LANES), F32)
    for group in range(GROUPS):
        columns = slice(group * SPAN, (group + 1) * SPAN)
        mine = owner == group
        high_part = jnp.where(mine, high, jnp.zeros_like(high))
        low_part = jnp.where(mine, low, jnp.zeros_like(low))
        acc = acc + jnp.dot(high_ref[:, columns], high_part, preferred_element_type=F32)
        acc = acc + jnp.dot(high_ref[:, columns], low_part, preferred_element_type=F32)
        acc = acc + jnp.dot(low_ref[:, columns], high_part, preferred_element_type=F32)
    local_ref[...] = acc[0:SPAN]
    state_ref[...] = jnp.broadcast_to(
        acc[SPAN:].astype(BF16)[None], (PEERS, ORDER, LANES)
    )


def output_kernel(states_ref, decay_ref, reach_ref, query_ref, signal_ref, local_ref, gain_ref, out_ref):
    half, core = lax.axis_index("z0"), lax.axis_index("core")
    lanes = pl.ds(pl.multiple_of(half * LANES, LANES), LANES)
    low = iota((ORDER, LANES), 1) < SIDE
    place = 4 * lax.axis_index("zh") + lax.axis_index("yh") + jnp.where(low, 0, 2)
    decay = decay_ref[...]
    carry = jnp.zeros((ORDER, LANES), F32)
    for block in range(2 * PEERS - 1):
        outer, odd, yh = block // 4, block // 2 % 2, block % 2
        state = states_ref[outer * 2 + yh].astype(F32)
        other = pltpu.roll(state, SIDE, 1)
        state = jnp.where(low, other, state) if odd else jnp.where(low, state, other)
        carry = jnp.where(block < place, carry * decay + state, carry)
    tiled = jnp.concatenate([carry] * GROUPS, axis=0)
    shape = (GROUPS * ORDER, LANES)
    tiled = jnp.where(iota(shape, 0) // ORDER == iota(shape, 1) % SIDE // FGROUP, tiled, 0.0)
    conv = local_ref[...] + exact_dot(reach_ref[...], tiled, ((1,), (0,)))
    gain = jnp.broadcast_to(gain_ref[0:1, lanes], (8, LANES))
    gain, _ = side_by_side(gain, gain, core)
    mixed = query_ref[...] * (conv + gain[0:1] * signal_ref[...])
    for run, value in enumerate((mixed, pltpu.roll(mixed, SIDE, 1))):
        value = value[:, 0:SIDE].astype(BF16)
        for part in range(2):
            out_ref[run, part] = value[part * ROWS : (part + 1) * ROWS]


def call(kernel, shapes, *operands, scratch=(), limit=16):
    return pl.pallas_call(
        kernel,
        out_shape=[jax.ShapeDtypeStruct(shape, dtype) for shape, dtype in shapes],
        in_specs=[pl.BlockSpec(memory_space=pltpu.VMEM)] * len(operands),
        out_specs=[pl.BlockSpec(memory_space=pltpu.VMEM)] * len(shapes),
        scratch_shapes=list(scratch),
        compiler_params=pltpu.CompilerParams(vmem_limit_bytes=limit << 20),
    )(*operands)


def ring_shift(block, distance):
    return lax.ppermute(block, "zh", [(i, (i + distance) % RING) for i in range(RING)])


def per_device(sequence, in_weight, short_taps, decay_rates, residues, skip_gain):
    halves = [in_weight[:, :, side * LANES : (side + 1) * LANES] for side in range(2)]
    slots = jnp.stack([halves[0], halves[0], halves[1], halves[1]])
    block = lax.all_to_all(slots, ("z0", "yh"), 0, 0, tiled=True)
    blocks = [None] * RING
    blocks[0] = block
    up, down = block, block
    for step in range(1, RING // 2 + 1):
        up = ring_shift(up, 1)
        blocks[step] = up
        if step < RING // 2:
            down = ring_shift(down, -1)
            blocks[RING - step] = down
    count = 64
    dealt, edge = call(deal_kernel, [((2, ROWS, DEPTH), BF16), ((2, HALO, DEPTH), BF16)], sequence)
    edge = lax.ppermute(edge, CTX, [(i, i + 1) for i in range(count - 1)])
    (slots,) = call(near_kernel, [((2, 2, HALO + ROWS, DEPTH), BF16)], edge, dealt)
    near = lax.all_to_all(slots.reshape(4, HALO + ROWS, DEPTH), ("z0", "core"), 0, 0, tiled=True)
    (slots,) = call(
        fan_kernel, [((RING, 2, HALO + SPAN, DEPTH), BF16)], near.reshape(2, 2, HALO + ROWS, DEPTH)
    )
    whole = lax.all_to_all(slots, CHAN, 0, 0, tiled=True)

    high, low, reach, decay = call(
        filter_kernel,
        [
            ((SPAN + ORDER, GROUPS * SPAN), BF16),
            ((SPAN + ORDER, GROUPS * SPAN), BF16),
            ((SPAN, GROUPS * ORDER), F32),
            ((ORDER, LANES), F32),
        ],
        decay_rates,
        residues,
    )
    (sums,) = call(
        early_kernel, [((2, HALO + SPAN, COLS), F32)], whole, *[blocks[step] for step in FIRST]
    )
    keep, send = call(
        late_kernel, [((HALO + SPAN, COLS), F32)] * 2, whole, sums, *[blocks[step] for step in LAST]
    )
    recv = lax.ppermute(send, "core", [(0, 1), (1, 0)])
    query, signal, local, states = call(
        scan_kernel,
        [((SPAN, LANES), F32)] * 3 + [((PEERS, ORDER, LANES), BF16)],
        keep,
        recv,
        short_taps,
        high,
        low,
        scratch=[pltpu.VMEM((HALO + SPAN, COLS), F32)],
    )
    states = lax.all_to_all(states, ("zh", "yh"), 0, 0, tiled=True)
    (slots,) = call(
        output_kernel,
        [((2, 2, ROWS, SIDE), BF16)],
        states,
        decay,
        reach,
        query,
        signal,
        local,
        skip_gain[None],
    )
    slots = lax.all_to_all(slots.reshape(4, ROWS, SIDE), ("z0", "core"), 0, 0, tiled=True)
    return slots.transpose(1, 0, 2).reshape(ROWS, 4 * SIDE)


def solution(mesh):
    fine = Mesh(mesh.devices.reshape(SIZES), AXES)
    return jax.shard_map(
        per_device,
        mesh=fine,
        in_specs=(
            P(CTX, CHAN),
            P(None, CTX, CHAN),
            P(None, None, CHAN),
            P(CHAN, None),
            P(CHAN, None),
            P(CHAN),
        ),
        out_specs=P(CTX, CHAN),
        check_vma=False,
    )
```

```python
import jax
import jax.numpy as jnp
from jax import lax
from jax.experimental import pallas as pl
from jax.experimental.pallas import tpu as pltpu
from jax.sharding import Mesh
from jax.sharding import PartitionSpec as P


AXES = ("zh", "z0", "yh", "core", "x", "yl")
SIZES = (8, 2, 2, 2, 4, 2)
CTX = ("zh", "z0", "yh", "core")
CHAN = ("x", "yl")
RING = 8

ROWS = 128
HALO = 16
SPAN = 256
LANES = 128
SIDE = 64
GROUPS = 4
FGROUP = 16
ORDER = 16
TAPS = 7
COLS = 3 * LANES
DEPTH = 256
PEERS = 16
HIGHEST = lax.Precision.HIGHEST
F32 = jnp.float32
BF16 = jnp.bfloat16


def iota(shape, axis):
    return lax.broadcasted_iota(jnp.int32, shape, axis)


def exact_dot(a, b, dims):
    return lax.dot_general(a, b, (dims, ((), ())), precision=HIGHEST, preferred_element_type=F32)


def side_by_side(even, odd, core):
    low = iota(even.shape, 1) < SIDE
    lower = jnp.where(low, even, pltpu.roll(odd, SIDE, 1))
    upper = jnp.where(low, pltpu.roll(even, SIDE, 1), odd)
    if isinstance(core, int):
        return (upper, lower) if core else (lower, upper)
    return jnp.where(core == 0, lower, upper), jnp.where(core == 0, upper, lower)


def own_filters(ref, half, core):
    rows = ref[pl.ds(pl.multiple_of(half * 2 * GROUPS, 2 * GROUPS), 2 * GROUPS), :]
    return jnp.where(core == 0, rows[0:GROUPS], rows[GROUPS:])


def filter_kernel(rates_ref, residues_ref, high_ref, low_ref, reach_ref, decay_ref):
    half, core = lax.axis_index("z0"), lax.axis_index("core")
    rates = own_filters(rates_ref, half, core)
    weights = own_filters(residues_ref, half, core) * jnp.sqrt(2.0 * rates)
    slot = iota((GROUPS, SPAN), 1)
    lag = jnp.where(slot == 0, 0, SPAN - slot).astype(F32)
    impulse = jnp.zeros((GROUPS, SPAN), F32)
    for mode in range(ORDER):
        impulse = impulse + weights[:, mode : mode + 1] * jnp.exp(
            -rates[:, mode : mode + 1] * lag
        )
    causal = iota((SPAN, SPAN), 0) >= iota((SPAN, SPAN), 1)
    left = (SPAN - 1 - iota((ORDER, SPAN), 1)).astype(F32)
    for group in range(GROUPS):
        columns = slice(group * SPAN, (group + 1) * SPAN)
        spread = jnp.broadcast_to(impulse[group : group + 1, :], (SPAN, SPAN))
        rolled = pltpu.roll(spread, 0, 1, stride=1, stride_axis=0)
        toeplitz = jnp.where(causal, rolled, 0.0)
        high = toeplitz.astype(BF16)
        high_ref[0:SPAN, columns] = high
        low_ref[0:SPAN, columns] = (toeplitz - high.astype(F32)).astype(BF16)
        pick = (iota((GROUPS, SPAN), 0) == group).astype(F32)
        state = jnp.exp(-exact_dot(rates, pick, ((0,), (0,))) * left)
        high = state.astype(BF16)
        high_ref[SPAN : SPAN + ORDER, columns] = high
        low_ref[SPAN : SPAN + ORDER, columns] = (state - high.astype(F32)).astype(BF16)
    shape = (GROUPS, GROUPS * ORDER)
    mode_pick = iota((ORDER, shape[1]), 0) == iota((ORDER, shape[1]), 1) % ORDER
    own = iota(shape, 0) == iota(shape, 1) // ORDER

    def flat(values):
        wide = exact_dot(values, mode_pick.astype(F32), ((1,), (0,)))
        return jnp.sum(jnp.where(own, wide, 0.0), axis=0, keepdims=True)

    ahead = (iota((SPAN, shape[1]), 0) + 1).astype(F32)
    reach_ref[...] = flat(weights) * jnp.exp(-flat(rates) * ahead)
    lanes = iota((GROUPS, LANES), 1) % SIDE // FGROUP == iota((GROUPS, LANES), 0)
    decay_ref[...] = jnp.exp(-float(SPAN) * exact_dot(rates, lanes.astype(F32), ((0,), (0,))))


def deal_kernel(rows_ref, out_ref, edge_ref):
    rows = rows_ref[...].astype(F32)
    for pair in range(DEPTH // LANES):
        first = 2 * pair * LANES
        even = rows[:, first : first + LANES]
        odd = rows[:, first + LANES : first + 2 * LANES]
        columns = slice(pair * LANES, (pair + 1) * LANES)
        for core, value in enumerate(side_by_side(even, odd, 0)):
            value = value.astype(BF16)
            out_ref[core, :, columns] = value
            edge_ref[core, :, columns] = value[ROWS - HALO :]


def near_kernel(edge_ref, dealt_ref, out_ref):
    for run in range(2):
        out_ref[run, :, 0:HALO, :] = edge_ref[...]
        out_ref[run, :, HALO:, :] = dealt_ref[...]


def fan_kernel(near_ref, out_ref):
    for run in range(2):
        first, second = near_ref[run, 0], near_ref[run, 1, HALO:, :]
        for target in range(RING):
            out_ref[target, run, 0 : HALO + ROWS, :] = first
            out_ref[target, run, HALO + ROWS :, :] = second


LAST = (RING // 2, RING // 2 + 1)
FIRST = tuple(step for step in range(RING) if step not in LAST)


def add_products(x_ref, blocks, steps, totals):
    here = lax.axis_index("zh")
    core = lax.axis_index("core")
    for step, block in zip(steps, blocks):
        source = lax.rem(here + jnp.where(core == 0, RING - step, step), RING)
        rows = [
            jnp.concatenate([block[near, part] for part in range(3)], axis=1)
            for near in range(4)
        ]
        weight = jnp.concatenate(rows, axis=0)
        totals = [
            total + jnp.dot(x_ref[source, group], weight, preferred_element_type=F32)
            for group, total in enumerate(totals)
        ]
    return totals


def early_kernel(x_ref, *refs):
    totals = [jnp.zeros((HALO + SPAN, COLS), F32)] * 2
    refs[-1][0], refs[-1][1] = add_products(x_ref, refs[:-1], FIRST, totals)


def late_kernel(x_ref, sums_ref, *refs):
    blocks, (keep_ref, send_ref) = refs[: len(LAST)], refs[len(LAST) :]
    core = lax.axis_index("core")
    even, odd = add_products(x_ref, blocks, LAST, [sums_ref[0], sums_ref[1]])
    for part in range(3):
        columns = slice(part * LANES, (part + 1) * LANES)
        keep_ref[:, columns], send_ref[:, columns] = side_by_side(
            even[:, columns], odd[:, columns], core
        )


def scan_kernel(
    keep_ref, recv_ref, taps_ref, high_ref, low_ref, query_ref, signal_ref, local_ref, state_ref, rows_ref
):
    half, core = lax.axis_index("z0"), lax.axis_index("core")
    lanes = pl.ds(pl.multiple_of(half * LANES, LANES), LANES)
    total = keep_ref[...] + recv_ref[...]
    rows_ref[...] = total.astype(BF16).astype(F32)
    filtered = []
    for part in range(3):
        columns = slice(part * LANES, (part + 1) * LANES)
        taps = taps_ref[part, :, lanes]
        taps, _ = side_by_side(taps, taps, core)
        value = jnp.zeros((SPAN, LANES), F32)
        for tap in range(TAPS):
            value = value + taps[tap : tap + 1, :] * rows_ref[
                HALO - tap : HALO - tap + SPAN, columns
            ]
        filtered.append(value)
    query_ref[...] = filtered[0]
    signal = filtered[1] * filtered[2]
    signal_ref[...] = signal
    high = signal.astype(BF16)
    low = (signal - high.astype(F32)).astype(BF16)
    owner = iota((SPAN, LANES), 1) % SIDE // FGROUP
    acc = jnp.zeros((SPAN + ORDER, LANES), F32)
    for group in range(GROUPS):
        columns = slice(group * SPAN, (group + 1) * SPAN)
        mine = owner == group
        high_part = jnp.where(mine, high, jnp.zeros_like(high))
        low_part = jnp.where(mine, low, jnp.zeros_like(low))
        acc = acc + jnp.dot(high_ref[:, columns], high_part, preferred_element_type=F32)
        acc = acc + jnp.dot(high_ref[:, columns], low_part, preferred_element_type=F32)
        acc = acc + jnp.dot(low_ref[:, columns], high_part, preferred_element_type=F32)
    local_ref[...] = acc[0:SPAN]
    state_ref[...] = jnp.broadcast_to(
        acc[SPAN:].astype(BF16)[None], (PEERS, ORDER, LANES)
    )


def output_kernel(states_ref, decay_ref, reach_ref, query_ref, signal_ref, local_ref, gain_ref, out_ref):
    half, core = lax.axis_index("z0"), lax.axis_index("core")
    lanes = pl.ds(pl.multiple_of(half * LANES, LANES), LANES)
    low = iota((ORDER, LANES), 1) < SIDE
    place = 4 * lax.axis_index("zh") + lax.axis_index("yh") + jnp.where(low, 0, 2)
    decay = decay_ref[...]
    carry = jnp.zeros((ORDER, LANES), F32)
    for block in range(2 * PEERS - 1):
        outer, odd, yh = block // 4, block // 2 % 2, block % 2
        state = states_ref[outer * 2 + yh].astype(F32)
        other = pltpu.roll(state, SIDE, 1)
        state = jnp.where(low, other, state) if odd else jnp.where(low, state, other)
        carry = jnp.where(block < place, carry * decay + state, carry)
    tiled = jnp.concatenate([carry] * GROUPS, axis=0)
    shape = (GROUPS * ORDER, LANES)
    tiled = jnp.where(iota(shape, 0) // ORDER == iota(shape, 1) % SIDE // FGROUP, tiled, 0.0)
    conv = local_ref[...] + exact_dot(reach_ref[...], tiled, ((1,), (0,)))
    gain = jnp.broadcast_to(gain_ref[0:1, lanes], (8, LANES))
    gain, _ = side_by_side(gain, gain, core)
    mixed = query_ref[...] * (conv + gain[0:1] * signal_ref[...])
    for run, value in enumerate((mixed, pltpu.roll(mixed, SIDE, 1))):
        value = value[:, 0:SIDE].astype(BF16)
        for part in range(2):
            out_ref[run, part] = value[part * ROWS : (part + 1) * ROWS]


def call(kernel, shapes, *operands, scratch=(), limit=16):
    return pl.pallas_call(
        kernel,
        out_shape=[jax.ShapeDtypeStruct(shape, dtype) for shape, dtype in shapes],
        in_specs=[pl.BlockSpec(memory_space=pltpu.VMEM)] * len(operands),
        out_specs=[pl.BlockSpec(memory_space=pltpu.VMEM)] * len(shapes),
        scratch_shapes=list(scratch),
        compiler_params=pltpu.CompilerParams(vmem_limit_bytes=limit << 20),
    )(*operands)


def ring_shift(block, distance):
    route = []
    for i in range(RING):
        for core in range(2):
            target = (i + (distance if core == 0 else -distance)) % RING
            route.append((2 * i + core, 2 * target + core))
    return lax.ppermute(block, ("zh", "core"), route)


def per_device(sequence, in_weight, short_taps, decay_rates, residues, skip_gain):
    halves = [in_weight[:, :, side * LANES : (side + 1) * LANES] for side in range(2)]
    slots = jnp.stack([halves[0], halves[0], halves[1], halves[1]])
    block = lax.all_to_all(slots, ("z0", "yh"), 0, 0, tiled=True)
    blocks = [None] * RING
    blocks[0] = block
    up, down = block, block
    for step in range(1, RING // 2 + 1):
        up = ring_shift(up, 1)
        blocks[step] = up
        if step < RING // 2:
            down = ring_shift(down, -1)
            blocks[RING - step] = down
    count = 64
    dealt, edge = call(deal_kernel, [((2, ROWS, DEPTH), BF16), ((2, HALO, DEPTH), BF16)], sequence)
    edge = lax.ppermute(edge, CTX, [(i, i + 1) for i in range(count - 1)])
    (slots,) = call(near_kernel, [((2, 2, HALO + ROWS, DEPTH), BF16)], edge, dealt)
    near = lax.all_to_all(slots.reshape(4, HALO + ROWS, DEPTH), ("z0", "core"), 0, 0, tiled=True)
    (slots,) = call(
        fan_kernel, [((RING, 2, HALO + SPAN, DEPTH), BF16)], near.reshape(2, 2, HALO + ROWS, DEPTH)
    )
    whole = lax.all_to_all(slots, CHAN, 0, 0, tiled=True)

    high, low, reach, decay = call(
        filter_kernel,
        [
            ((SPAN + ORDER, GROUPS * SPAN), BF16),
            ((SPAN + ORDER, GROUPS * SPAN), BF16),
            ((SPAN, GROUPS * ORDER), F32),
            ((ORDER, LANES), F32),
        ],
        decay_rates,
        residues,
    )
    (sums,) = call(
        early_kernel, [((2, HALO + SPAN, COLS), F32)], whole, *[blocks[step] for step in FIRST]
    )
    keep, send = call(
        late_kernel, [((HALO + SPAN, COLS), F32)] * 2, whole, sums, *[blocks[step] for step in LAST]
    )
    recv = lax.ppermute(send, "core", [(0, 1), (1, 0)])
    query, signal, local, states = call(
        scan_kernel,
        [((SPAN, LANES), F32)] * 3 + [((PEERS, ORDER, LANES), BF16)],
        keep,
        recv,
        short_taps,
        high,
        low,
        scratch=[pltpu.VMEM((HALO + SPAN, COLS), F32)],
    )
    states = lax.all_to_all(states, ("zh", "yh"), 0, 0, tiled=True)
    (slots,) = call(
        output_kernel,
        [((2, 2, ROWS, SIDE), BF16)],
        states,
        decay,
        reach,
        query,
        signal,
        local,
        skip_gain[None],
    )
    slots = lax.all_to_all(slots.reshape(4, ROWS, SIDE), ("z0", "core"), 0, 0, tiled=True)
    return slots.transpose(1, 0, 2).reshape(ROWS, 4 * SIDE)


def solution(mesh):
    fine = Mesh(mesh.devices.reshape(SIZES), AXES)
    return jax.shard_map(
        per_device,
        mesh=fine,
        in_specs=(
            P(CTX, CHAN),
            P(None, CTX, CHAN),
            P(None, None, CHAN),
            P(CHAN, None),
            P(CHAN, None),
            P(CHAN),
        ),
        out_specs=P(CTX, CHAN),
        check_vma=False,
    )
```

```python
import jax
import jax.numpy as jnp
from jax import lax
from jax.experimental import pallas as pl
from jax.experimental.pallas import tpu as pltpu
from jax.sharding import Mesh
from jax.sharding import PartitionSpec as P


AXES = ("zh", "z0", "yh", "core", "x", "yl")
SIZES = (8, 2, 2, 2, 4, 2)
CTX = ("zh", "z0", "yh", "core")
CHAN = ("x", "yl")
RING = 8

ROWS = 128
HALO = 16
SPAN = 256
LANES = 128
SIDE = 64
GROUPS = 4
FGROUP = 16
ORDER = 16
TAPS = 7
COLS = 3 * LANES
DEPTH = 256
PEERS = 16
HIGHEST = lax.Precision.HIGHEST
F32 = jnp.float32
BF16 = jnp.bfloat16


def iota(shape, axis):
    return lax.broadcasted_iota(jnp.int32, shape, axis)


def exact_dot(a, b, dims):
    return lax.dot_general(a, b, (dims, ((), ())), precision=HIGHEST, preferred_element_type=F32)


def side_by_side(even, odd, core):
    low = iota(even.shape, 1) < SIDE
    lower = jnp.where(low, even, pltpu.roll(odd, SIDE, 1))
    upper = jnp.where(low, pltpu.roll(even, SIDE, 1), odd)
    if isinstance(core, int):
        return (upper, lower) if core else (lower, upper)
    return jnp.where(core == 0, lower, upper), jnp.where(core == 0, upper, lower)


def own_filters(ref, half, core):
    rows = ref[pl.ds(pl.multiple_of(half * 2 * GROUPS, 2 * GROUPS), 2 * GROUPS), :]
    return jnp.where(core == 0, rows[0:GROUPS], rows[GROUPS:])


def filter_kernel(rates_ref, residues_ref, high_ref, low_ref, reach_ref, decay_ref):
    half, core = lax.axis_index("z0"), lax.axis_index("core")
    rates = own_filters(rates_ref, half, core)
    weights = own_filters(residues_ref, half, core) * jnp.sqrt(2.0 * rates)
    slot = iota((GROUPS, SPAN), 1)
    lag = jnp.where(slot == 0, 0, SPAN - slot).astype(F32)
    impulse = jnp.zeros((GROUPS, SPAN), F32)
    for mode in range(ORDER):
        impulse = impulse + weights[:, mode : mode + 1] * jnp.exp(
            -rates[:, mode : mode + 1] * lag
        )
    causal = iota((SPAN, SPAN), 0) >= iota((SPAN, SPAN), 1)
    left = (SPAN - 1 - iota((ORDER, SPAN), 1)).astype(F32)
    for group in range(GROUPS):
        columns = slice(group * SPAN, (group + 1) * SPAN)
        spread = jnp.broadcast_to(impulse[group : group + 1, :], (SPAN, SPAN))
        rolled = pltpu.roll(spread, 0, 1, stride=1, stride_axis=0)
        toeplitz = jnp.where(causal, rolled, 0.0)
        high = toeplitz.astype(BF16)
        high_ref[0:SPAN, columns] = high
        low_ref[0:SPAN, columns] = (toeplitz - high.astype(F32)).astype(BF16)
        pick = (iota((GROUPS, SPAN), 0) == group).astype(F32)
        state = jnp.exp(-exact_dot(rates, pick, ((0,), (0,))) * left)
        high = state.astype(BF16)
        high_ref[SPAN : SPAN + ORDER, columns] = high
        low_ref[SPAN : SPAN + ORDER, columns] = (state - high.astype(F32)).astype(BF16)
    shape = (GROUPS, GROUPS * ORDER)
    mode_pick = iota((ORDER, shape[1]), 0) == iota((ORDER, shape[1]), 1) % ORDER
    own = iota(shape, 0) == iota(shape, 1) // ORDER

    def flat(values):
        wide = exact_dot(values, mode_pick.astype(F32), ((1,), (0,)))
        return jnp.sum(jnp.where(own, wide, 0.0), axis=0, keepdims=True)

    ahead = (iota((SPAN, shape[1]), 0) + 1).astype(F32)
    reach_ref[...] = flat(weights) * jnp.exp(-flat(rates) * ahead)
    lanes = iota((GROUPS, LANES), 1) % SIDE // FGROUP == iota((GROUPS, LANES), 0)
    decay_ref[...] = jnp.exp(-float(SPAN) * exact_dot(rates, lanes.astype(F32), ((0,), (0,))))


def deal_kernel(rows_ref, out_ref, edge_ref):
    rows = rows_ref[...].astype(F32)
    for pair in range(DEPTH // LANES):
        first = 2 * pair * LANES
        even = rows[:, first : first + LANES]
        odd = rows[:, first + LANES : first + 2 * LANES]
        columns = slice(pair * LANES, (pair + 1) * LANES)
        for core, value in enumerate(side_by_side(even, odd, 0)):
            value = value.astype(BF16)
            out_ref[core, :, columns] = value
            edge_ref[core, :, columns] = value[ROWS - HALO :]


def near_kernel(edge_ref, dealt_ref, out_ref):
    for run in range(2):
        out_ref[run, :, 0:HALO, :] = edge_ref[...]
        out_ref[run, :, HALO:, :] = dealt_ref[...]


def fan_kernel(near_ref, out_ref):
    for run in range(2):
        first, second = near_ref[run, 0], near_ref[run, 1, HALO:, :]
        for target in range(RING):
            out_ref[target, run, 0 : HALO + ROWS, :] = first
            out_ref[target, run, HALO + ROWS :, :] = second


LAST = (RING // 2, RING // 2 + 1)
FIRST = tuple(step for step in range(RING) if step not in LAST)


def add_products(x_ref, blocks, steps, totals):
    here = lax.axis_index("zh")
    core = lax.axis_index("core")
    for step, block in zip(steps, blocks):
        source = lax.rem(here + jnp.where(core == 0, RING - step, step), RING)
        slot = jnp.where(core == 0, source, RING - 1 - source)
        rows = [
            jnp.concatenate([block[near, part] for part in range(3)], axis=1)
            for near in range(4)
        ]
        weight = jnp.concatenate(rows, axis=0)
        totals = [
            total + jnp.dot(x_ref[slot, group], weight, preferred_element_type=F32)
            for group, total in enumerate(totals)
        ]
    return totals


def early_kernel(x_ref, *refs):
    totals = [jnp.zeros((HALO + SPAN, COLS), F32)] * 2
    refs[-1][0], refs[-1][1] = add_products(x_ref, refs[:-1], FIRST, totals)


def late_kernel(x_ref, sums_ref, *refs):
    blocks, (keep_ref, send_ref) = refs[: len(LAST)], refs[len(LAST) :]
    core = lax.axis_index("core")
    even, odd = add_products(x_ref, blocks, LAST, [sums_ref[0], sums_ref[1]])
    for part in range(3):
        columns = slice(part * LANES, (part + 1) * LANES)
        keep_ref[:, columns], send_ref[:, columns] = side_by_side(
            even[:, columns], odd[:, columns], core
        )


def scan_kernel(
    keep_ref, recv_ref, taps_ref, high_ref, low_ref, query_ref, signal_ref, local_ref, state_ref, rows_ref
):
    half, core = lax.axis_index("z0"), lax.axis_index("core")
    lanes = pl.ds(pl.multiple_of(half * LANES, LANES), LANES)
    total = keep_ref[...] + recv_ref[...]
    rows_ref[...] = total.astype(BF16).astype(F32)
    filtered = []
    for part in range(3):
        columns = slice(part * LANES, (part + 1) * LANES)
        taps = taps_ref[part, :, lanes]
        taps, _ = side_by_side(taps, taps, core)
        value = jnp.zeros((SPAN, LANES), F32)
        for tap in range(TAPS):
            value = value + taps[tap : tap + 1, :] * rows_ref[
                HALO - tap : HALO - tap + SPAN, columns
            ]
        filtered.append(value)
    query_ref[...] = filtered[0]
    signal = filtered[1] * filtered[2]
    signal_ref[...] = signal
    high = signal.astype(BF16)
    low = (signal - high.astype(F32)).astype(BF16)
    owner = iota((SPAN, LANES), 1) % SIDE // FGROUP
    acc = jnp.zeros((SPAN + ORDER, LANES), F32)
    for group in range(GROUPS):
        columns = slice(group * SPAN, (group + 1) * SPAN)
        mine = owner == group
        high_part = jnp.where(mine, high, jnp.zeros_like(high))
        low_part = jnp.where(mine, low, jnp.zeros_like(low))
        acc = acc + jnp.dot(high_ref[:, columns], high_part, preferred_element_type=F32)
        acc = acc + jnp.dot(high_ref[:, columns], low_part, preferred_element_type=F32)
        acc = acc + jnp.dot(low_ref[:, columns], high_part, preferred_element_type=F32)
    local_ref[...] = acc[0:SPAN]
    state_ref[...] = jnp.broadcast_to(
        acc[SPAN:].astype(BF16)[None], (PEERS, ORDER, LANES)
    )


def output_kernel(states_ref, decay_ref, reach_ref, query_ref, signal_ref, local_ref, gain_ref, out_ref):
    half, core = lax.axis_index("z0"), lax.axis_index("core")
    lanes = pl.ds(pl.multiple_of(half * LANES, LANES), LANES)
    low = iota((ORDER, LANES), 1) < SIDE
    place = 4 * lax.axis_index("zh") + lax.axis_index("yh") + jnp.where(low, 0, 2)
    decay = decay_ref[...]
    carry = jnp.zeros((ORDER, LANES), F32)
    for block in range(2 * PEERS - 1):
        outer, odd, yh = block // 4, block // 2 % 2, block % 2
        state = states_ref[outer * 2 + yh].astype(F32)
        other = pltpu.roll(state, SIDE, 1)
        state = jnp.where(low, other, state) if odd else jnp.where(low, state, other)
        carry = jnp.where(block < place, carry * decay + state, carry)
    tiled = jnp.concatenate([carry] * GROUPS, axis=0)
    shape = (GROUPS * ORDER, LANES)
    tiled = jnp.where(iota(shape, 0) // ORDER == iota(shape, 1) % SIDE // FGROUP, tiled, 0.0)
    conv = local_ref[...] + exact_dot(reach_ref[...], tiled, ((1,), (0,)))
    gain = jnp.broadcast_to(gain_ref[0:1, lanes], (8, LANES))
    gain, _ = side_by_side(gain, gain, core)
    mixed = query_ref[...] * (conv + gain[0:1] * signal_ref[...])
    for run, value in enumerate((mixed, pltpu.roll(mixed, SIDE, 1))):
        value = value[:, 0:SIDE].astype(BF16)
        for part in range(2):
            out_ref[run, part] = value[part * ROWS : (part + 1) * ROWS]


def call(kernel, shapes, *operands, scratch=(), limit=16):
    return pl.pallas_call(
        kernel,
        out_shape=[jax.ShapeDtypeStruct(shape, dtype) for shape, dtype in shapes],
        in_specs=[pl.BlockSpec(memory_space=pltpu.VMEM)] * len(operands),
        out_specs=[pl.BlockSpec(memory_space=pltpu.VMEM)] * len(shapes),
        scratch_shapes=list(scratch),
        compiler_params=pltpu.CompilerParams(vmem_limit_bytes=limit << 20),
    )(*operands)


def ring_shift(block, distance):
    route = []
    for i in range(RING):
        for core in range(2):
            target = (i + (distance if core == 0 else -distance)) % RING
            route.append((2 * i + core, 2 * target + core))
    return lax.ppermute(block, ("zh", "core"), route)


def per_device(sequence, in_weight, short_taps, decay_rates, residues, skip_gain):
    halves = [in_weight[:, :, side * LANES : (side + 1) * LANES] for side in range(2)]
    slots = jnp.stack([halves[0], halves[0], halves[1], halves[1]])
    block = lax.all_to_all(slots, ("z0", "yh"), 0, 0, tiled=True)
    blocks = [None] * RING
    blocks[0] = block
    up, down = block, block
    for step in range(1, RING // 2 + 1):
        up = ring_shift(up, 1)
        blocks[step] = up
        if step < RING // 2:
            down = ring_shift(down, -1)
            blocks[RING - step] = down
    count = 64
    dealt, edge = call(deal_kernel, [((2, ROWS, DEPTH), BF16), ((2, HALO, DEPTH), BF16)], sequence)
    edge = lax.ppermute(edge, CTX, [(i, i + 1) for i in range(count - 1)])
    (slots,) = call(near_kernel, [((2, 2, HALO + ROWS, DEPTH), BF16)], edge, dealt)
    near = lax.all_to_all(slots.reshape(4, HALO + ROWS, DEPTH), ("z0", "core"), 0, 0, tiled=True)
    (slots,) = call(
        fan_kernel, [((RING, 2, HALO + SPAN, DEPTH), BF16)], near.reshape(2, 2, HALO + ROWS, DEPTH)
    )
    peers = [list(range(RING)), list(range(2 * RING - 1, RING - 1, -1))]
    whole = lax.all_to_all(
        slots, ("core",) + CHAN, 0, 0, axis_index_groups=peers, tiled=True
    )

    high, low, reach, decay = call(
        filter_kernel,
        [
            ((SPAN + ORDER, GROUPS * SPAN), BF16),
            ((SPAN + ORDER, GROUPS * SPAN), BF16),
            ((SPAN, GROUPS * ORDER), F32),
            ((ORDER, LANES), F32),
        ],
        decay_rates,
        residues,
    )
    (sums,) = call(
        early_kernel, [((2, HALO + SPAN, COLS), F32)], whole, *[blocks[step] for step in FIRST]
    )
    keep, send = call(
        late_kernel, [((HALO + SPAN, COLS), F32)] * 2, whole, sums, *[blocks[step] for step in LAST]
    )
    recv = lax.ppermute(send, "core", [(0, 1), (1, 0)])
    query, signal, local, states = call(
        scan_kernel,
        [((SPAN, LANES), F32)] * 3 + [((PEERS, ORDER, LANES), BF16)],
        keep,
        recv,
        short_taps,
        high,
        low,
        scratch=[pltpu.VMEM((HALO + SPAN, COLS), F32)],
    )
    states = lax.all_to_all(states, ("zh", "yh"), 0, 0, tiled=True)
    (slots,) = call(
        output_kernel,
        [((2, 2, ROWS, SIDE), BF16)],
        states,
        decay,
        reach,
        query,
        signal,
        local,
        skip_gain[None],
    )
    slots = lax.all_to_all(slots.reshape(4, ROWS, SIDE), ("z0", "core"), 0, 0, tiled=True)
    return slots.transpose(1, 0, 2).reshape(ROWS, 4 * SIDE)


def solution(mesh):
    fine = Mesh(mesh.devices.reshape(SIZES), AXES)
    return jax.shard_map(
        per_device,
        mesh=fine,
        in_specs=(
            P(CTX, CHAN),
            P(None, CTX, CHAN),
            P(None, None, CHAN),
            P(CHAN, None),
            P(CHAN, None),
            P(CHAN),
        ),
        out_specs=P(CTX, CHAN),
        check_vma=False,
    )
```

```python
import jax
import jax.numpy as jnp
from jax import lax
from jax.experimental import pallas as pl
from jax.experimental.pallas import tpu as pltpu
from jax.sharding import Mesh
from jax.sharding import PartitionSpec as P


AXES = ("zh", "z0", "yh", "core", "x", "yl")
SIZES = (8, 2, 2, 2, 4, 2)
CTX = ("zh", "z0", "yh", "core")
CHAN = ("x", "yl")
RING = 8

ROWS = 128
HALO = 16
SPAN = 256
LANES = 128
SIDE = 64
GROUPS = 4
FGROUP = 16
ORDER = 16
TAPS = 7
COLS = 3 * LANES
DEPTH = 256
PEERS = 16
HIGHEST = lax.Precision.HIGHEST
F32 = jnp.float32
BF16 = jnp.bfloat16


def iota(shape, axis):
    return lax.broadcasted_iota(jnp.int32, shape, axis)


def exact_dot(a, b, dims):
    return lax.dot_general(a, b, (dims, ((), ())), precision=HIGHEST, preferred_element_type=F32)


def side_by_side(even, odd, core):
    low = iota(even.shape, 1) < SIDE
    lower = jnp.where(low, even, pltpu.roll(odd, SIDE, 1))
    upper = jnp.where(low, pltpu.roll(even, SIDE, 1), odd)
    if isinstance(core, int):
        return (upper, lower) if core else (lower, upper)
    return jnp.where(core == 0, lower, upper), jnp.where(core == 0, upper, lower)


def own_filters(ref, half, core):
    rows = ref[pl.ds(pl.multiple_of(half * 2 * GROUPS, 2 * GROUPS), 2 * GROUPS), :]
    return jnp.where(core == 0, rows[0:GROUPS], rows[GROUPS:])


def filter_kernel(rates_ref, residues_ref, high_ref, low_ref, reach_ref, decay_ref):
    half, core = lax.axis_index("z0"), lax.axis_index("core")
    rates = own_filters(rates_ref, half, core)
    weights = own_filters(residues_ref, half, core) * jnp.sqrt(2.0 * rates)
    slot = iota((GROUPS, SPAN), 1)
    lag = jnp.where(slot == 0, 0, SPAN - slot).astype(F32)
    impulse = jnp.zeros((GROUPS, SPAN), F32)
    for mode in range(ORDER):
        impulse = impulse + weights[:, mode : mode + 1] * jnp.exp(
            -rates[:, mode : mode + 1] * lag
        )
    causal = iota((SPAN, SPAN), 0) >= iota((SPAN, SPAN), 1)
    left = (SPAN - 1 - iota((ORDER, SPAN), 1)).astype(F32)
    for group in range(GROUPS):
        columns = slice(group * SPAN, (group + 1) * SPAN)
        spread = jnp.broadcast_to(impulse[group : group + 1, :], (SPAN, SPAN))
        rolled = pltpu.roll(spread, 0, 1, stride=1, stride_axis=0)
        toeplitz = jnp.where(causal, rolled, 0.0)
        high = toeplitz.astype(BF16)
        high_ref[0:SPAN, columns] = high
        low_ref[0:SPAN, columns] = (toeplitz - high.astype(F32)).astype(BF16)
        pick = (iota((GROUPS, SPAN), 0) == group).astype(F32)
        state = jnp.exp(-exact_dot(rates, pick, ((0,), (0,))) * left)
        high = state.astype(BF16)
        high_ref[SPAN : SPAN + ORDER, columns] = high
        low_ref[SPAN : SPAN + ORDER, columns] = (state - high.astype(F32)).astype(BF16)
    shape = (GROUPS, GROUPS * ORDER)
    mode_pick = iota((ORDER, shape[1]), 0) == iota((ORDER, shape[1]), 1) % ORDER
    own = iota(shape, 0) == iota(shape, 1) // ORDER

    def flat(values):
        wide = exact_dot(values, mode_pick.astype(F32), ((1,), (0,)))
        return jnp.sum(jnp.where(own, wide, 0.0), axis=0, keepdims=True)

    ahead = (iota((SPAN, shape[1]), 0) + 1).astype(F32)
    reach_ref[...] = flat(weights) * jnp.exp(-flat(rates) * ahead)
    lanes = iota((GROUPS, LANES), 1) % SIDE // FGROUP == iota((GROUPS, LANES), 0)
    decay_ref[...] = jnp.exp(-float(SPAN) * exact_dot(rates, lanes.astype(F32), ((0,), (0,))))


def deal_kernel(rows_ref, out_ref, edge_ref):
    rows = rows_ref[...].astype(F32)
    for pair in range(DEPTH // LANES):
        first = 2 * pair * LANES
        even = rows[:, first : first + LANES]
        odd = rows[:, first + LANES : first + 2 * LANES]
        columns = slice(pair * LANES, (pair + 1) * LANES)
        for core, value in enumerate(side_by_side(even, odd, 0)):
            value = value.astype(BF16)
            out_ref[core, :, columns] = value
            edge_ref[core, :, columns] = value[ROWS - HALO :]


def near_kernel(edge_ref, dealt_ref, out_ref):
    for run in range(2):
        out_ref[run, :, 0:HALO, :] = edge_ref[...]
        out_ref[run, :, HALO:, :] = dealt_ref[...]


def fan_kernel(near_ref, out_ref):
    for run in range(2):
        first, second = near_ref[run, 0], near_ref[run, 1, HALO:, :]
        for target in range(RING):
            out_ref[target, run, 0 : HALO + ROWS, :] = first
            out_ref[target, run, HALO + ROWS :, :] = second


LAST = (RING // 2, RING // 2 + 1)
FIRST = tuple(step for step in range(RING) if step not in LAST)


def add_products(x_ref, blocks, steps, totals):
    here = lax.axis_index("zh")
    core = lax.axis_index("core")
    for step, block in zip(steps, blocks):
        source = lax.rem(here + jnp.where(core == 0, RING - step, step), RING)
        slot = jnp.where(core == 0, source, RING - 1 - source)
        rows = [
            jnp.concatenate([block[near, part] for part in range(3)], axis=1)
            for near in range(4)
        ]
        weight = jnp.concatenate(rows, axis=0)
        totals = [
            total + jnp.dot(x_ref[slot, group], weight, preferred_element_type=F32)
            for group, total in enumerate(totals)
        ]
    return totals


def early_kernel(x_ref, *refs):
    totals = [jnp.zeros((HALO + SPAN, COLS), F32)] * 2
    refs[-1][0], refs[-1][1] = add_products(x_ref, refs[:-1], FIRST, totals)


def late_kernel(x_ref, sums_ref, *refs):
    blocks, (keep_ref, send_ref) = refs[: len(LAST)], refs[len(LAST) :]
    core = lax.axis_index("core")
    even, odd = add_products(x_ref, blocks, LAST, [sums_ref[0], sums_ref[1]])
    for part in range(3):
        columns = slice(part * LANES, (part + 1) * LANES)
        keep_ref[:, columns], send_ref[:, columns] = side_by_side(
            even[:, columns], odd[:, columns], core
        )


def scan_kernel(
    keep_ref, recv_ref, taps_ref, high_ref, low_ref, query_ref, signal_ref, local_ref, state_ref, rows_ref
):
    half, core = lax.axis_index("z0"), lax.axis_index("core")
    lanes = pl.ds(pl.multiple_of(half * LANES, LANES), LANES)
    total = keep_ref[...] + recv_ref[...]
    rows_ref[...] = total.astype(BF16).astype(F32)
    filtered = []
    for part in range(3):
        columns = slice(part * LANES, (part + 1) * LANES)
        taps = taps_ref[part, :, lanes]
        taps, _ = side_by_side(taps, taps, core)
        value = jnp.zeros((SPAN, LANES), F32)
        for tap in range(TAPS):
            value = value + taps[tap : tap + 1, :] * rows_ref[
                HALO - tap : HALO - tap + SPAN, columns
            ]
        filtered.append(value)
    query_ref[...] = filtered[0]
    signal = filtered[1] * filtered[2]
    signal_ref[...] = signal
    high = signal.astype(BF16)
    low = (signal - high.astype(F32)).astype(BF16)
    owner = iota((SPAN, LANES), 1) % SIDE // FGROUP
    acc = jnp.zeros((SPAN + ORDER, LANES), F32)
    for group in range(GROUPS):
        columns = slice(group * SPAN, (group + 1) * SPAN)
        mine = owner == group
        high_part = jnp.where(mine, high, jnp.zeros_like(high))
        low_part = jnp.where(mine, low, jnp.zeros_like(low))
        acc = acc + jnp.dot(high_ref[:, columns], high_part, preferred_element_type=F32)
        acc = acc + jnp.dot(high_ref[:, columns], low_part, preferred_element_type=F32)
        acc = acc + jnp.dot(low_ref[:, columns], high_part, preferred_element_type=F32)
    local_ref[...] = acc[0:SPAN]
    state_ref[...] = jnp.broadcast_to(
        acc[SPAN:].astype(BF16)[None], (PEERS, ORDER, LANES)
    )


def output_kernel(states_ref, decay_ref, reach_ref, query_ref, signal_ref, local_ref, gain_ref, out_ref):
    half, core = lax.axis_index("z0"), lax.axis_index("core")
    lanes = pl.ds(pl.multiple_of(half * LANES, LANES), LANES)
    low = iota((ORDER, LANES), 1) < SIDE
    place = 4 * lax.axis_index("zh") + lax.axis_index("yh") + jnp.where(low, 0, 2)
    decay = decay_ref[...]
    carry = jnp.zeros((ORDER, LANES), F32)
    for block in range(2 * PEERS - 1):
        outer, odd, yh = block // 4, block // 2 % 2, block % 2
        slot = outer * 2 + yh
        state = states_ref[jnp.where(core == 0, slot, PEERS - 1 - slot)].astype(F32)
        other = pltpu.roll(state, SIDE, 1)
        state = jnp.where(low, other, state) if odd else jnp.where(low, state, other)
        carry = jnp.where(block < place, carry * decay + state, carry)
    tiled = jnp.concatenate([carry] * GROUPS, axis=0)
    shape = (GROUPS * ORDER, LANES)
    tiled = jnp.where(iota(shape, 0) // ORDER == iota(shape, 1) % SIDE // FGROUP, tiled, 0.0)
    conv = local_ref[...] + exact_dot(reach_ref[...], tiled, ((1,), (0,)))
    gain = jnp.broadcast_to(gain_ref[0:1, lanes], (8, LANES))
    gain, _ = side_by_side(gain, gain, core)
    mixed = query_ref[...] * (conv + gain[0:1] * signal_ref[...])
    for run, value in enumerate((mixed, pltpu.roll(mixed, SIDE, 1))):
        value = value[:, 0:SIDE].astype(BF16)
        for part in range(2):
            out_ref[run, part] = value[part * ROWS : (part + 1) * ROWS]


def call(kernel, shapes, *operands, scratch=(), limit=16):
    return pl.pallas_call(
        kernel,
        out_shape=[jax.ShapeDtypeStruct(shape, dtype) for shape, dtype in shapes],
        in_specs=[pl.BlockSpec(memory_space=pltpu.VMEM)] * len(operands),
        out_specs=[pl.BlockSpec(memory_space=pltpu.VMEM)] * len(shapes),
        scratch_shapes=list(scratch),
        compiler_params=pltpu.CompilerParams(vmem_limit_bytes=limit << 20),
    )(*operands)


def ring_shift(block, distance):
    route = []
    for i in range(RING):
        for core in range(2):
            target = (i + (distance if core == 0 else -distance)) % RING
            route.append((2 * i + core, 2 * target + core))
    return lax.ppermute(block, ("zh", "core"), route)


def per_device(sequence, in_weight, short_taps, decay_rates, residues, skip_gain):
    halves = [in_weight[:, :, side * LANES : (side + 1) * LANES] for side in range(2)]
    slots = jnp.stack([halves[0], halves[0], halves[1], halves[1]])
    block = lax.all_to_all(slots, ("z0", "yh"), 0, 0, tiled=True)
    blocks = [None] * RING
    blocks[0] = block
    up, down = block, block
    for step in range(1, RING // 2 + 1):
        up = ring_shift(up, 1)
        blocks[step] = up
        if step < RING // 2:
            down = ring_shift(down, -1)
            blocks[RING - step] = down
    count = 64
    dealt, edge = call(deal_kernel, [((2, ROWS, DEPTH), BF16), ((2, HALO, DEPTH), BF16)], sequence)
    edge = lax.ppermute(edge, CTX, [(i, i + 1) for i in range(count - 1)])
    (slots,) = call(near_kernel, [((2, 2, HALO + ROWS, DEPTH), BF16)], edge, dealt)
    near = lax.all_to_all(slots.reshape(4, HALO + ROWS, DEPTH), ("z0", "core"), 0, 0, tiled=True)
    (slots,) = call(
        fan_kernel, [((RING, 2, HALO + SPAN, DEPTH), BF16)], near.reshape(2, 2, HALO + ROWS, DEPTH)
    )
    peers = [list(range(RING)), list(range(2 * RING - 1, RING - 1, -1))]
    whole = lax.all_to_all(
        slots, ("core",) + CHAN, 0, 0, axis_index_groups=peers, tiled=True
    )

    high, low, reach, decay = call(
        filter_kernel,
        [
            ((SPAN + ORDER, GROUPS * SPAN), BF16),
            ((SPAN + ORDER, GROUPS * SPAN), BF16),
            ((SPAN, GROUPS * ORDER), F32),
            ((ORDER, LANES), F32),
        ],
        decay_rates,
        residues,
    )
    (sums,) = call(
        early_kernel, [((2, HALO + SPAN, COLS), F32)], whole, *[blocks[step] for step in FIRST]
    )
    keep, send = call(
        late_kernel, [((HALO + SPAN, COLS), F32)] * 2, whole, sums, *[blocks[step] for step in LAST]
    )
    recv = lax.ppermute(send, "core", [(0, 1), (1, 0)])
    query, signal, local, states = call(
        scan_kernel,
        [((SPAN, LANES), F32)] * 3 + [((PEERS, ORDER, LANES), BF16)],
        keep,
        recv,
        short_taps,
        high,
        low,
        scratch=[pltpu.VMEM((HALO + SPAN, COLS), F32)],
    )
    peers = [list(range(PEERS)), list(range(2 * PEERS - 1, PEERS - 1, -1))]
    states = lax.all_to_all(
        states, ("core", "zh", "yh"), 0, 0, axis_index_groups=peers, tiled=True
    )
    (slots,) = call(
        output_kernel,
        [((2, 2, ROWS, SIDE), BF16)],
        states,
        decay,
        reach,
        query,
        signal,
        local,
        skip_gain[None],
    )
    slots = lax.all_to_all(slots.reshape(4, ROWS, SIDE), ("z0", "core"), 0, 0, tiled=True)
    return slots.transpose(1, 0, 2).reshape(ROWS, 4 * SIDE)


def solution(mesh):
    fine = Mesh(mesh.devices.reshape(SIZES), AXES)
    return jax.shard_map(
        per_device,
        mesh=fine,
        in_specs=(
            P(CTX, CHAN),
            P(None, CTX, CHAN),
            P(None, None, CHAN),
            P(CHAN, None),
            P(CHAN, None),
            P(CHAN),
        ),
        out_specs=P(CTX, CHAN),
        check_vma=False,
    )
```

```python
import jax
import jax.numpy as jnp
from jax import lax
from jax.experimental import pallas as pl
from jax.experimental.pallas import tpu as pltpu
from jax.sharding import Mesh
from jax.sharding import PartitionSpec as P


AXES = ("zh", "z0", "yh", "core", "x", "yl")
SIZES = (8, 2, 2, 2, 4, 2)
CTX = ("zh", "z0", "yh", "core")
CHAN = ("x", "yl")
RING = 8

ROWS = 128
HALO = 16
SPAN = 256
LANES = 128
SIDE = 64
GROUPS = 4
FGROUP = 16
ORDER = 16
TAPS = 7
COLS = 3 * LANES
DEPTH = 256
PEERS = 16
HIGHEST = lax.Precision.HIGHEST
F32 = jnp.float32
BF16 = jnp.bfloat16


def iota(shape, axis):
    return lax.broadcasted_iota(jnp.int32, shape, axis)


def exact_dot(a, b, dims):
    return lax.dot_general(a, b, (dims, ((), ())), precision=HIGHEST, preferred_element_type=F32)


def side_by_side(even, odd, core):
    low = iota(even.shape, 1) < SIDE
    lower = jnp.where(low, even, pltpu.roll(odd, SIDE, 1))
    upper = jnp.where(low, pltpu.roll(even, SIDE, 1), odd)
    if isinstance(core, int):
        return (upper, lower) if core else (lower, upper)
    return jnp.where(core == 0, lower, upper), jnp.where(core == 0, upper, lower)


def own_filters(ref, half, core):
    rows = ref[pl.ds(pl.multiple_of(half * 2 * GROUPS, 2 * GROUPS), 2 * GROUPS), :]
    return jnp.where(core == 0, rows[0:GROUPS], rows[GROUPS:])


def filter_kernel(rates_ref, residues_ref, high_ref, low_ref, reach_ref, decay_ref):
    half, core = lax.axis_index("z0"), lax.axis_index("core")
    rates = own_filters(rates_ref, half, core)
    weights = own_filters(residues_ref, half, core) * jnp.sqrt(2.0 * rates)
    slot = iota((GROUPS, SPAN), 1)
    lag = jnp.where(slot == 0, 0, SPAN - slot).astype(F32)
    impulse = jnp.zeros((GROUPS, SPAN), F32)
    for mode in range(ORDER):
        impulse = impulse + weights[:, mode : mode + 1] * jnp.exp(
            -rates[:, mode : mode + 1] * lag
        )
    causal = iota((SPAN, SPAN), 0) >= iota((SPAN, SPAN), 1)
    left = (SPAN - 1 - iota((ORDER, SPAN), 1)).astype(F32)
    for group in range(GROUPS):
        columns = slice(group * SPAN, (group + 1) * SPAN)
        spread = jnp.broadcast_to(impulse[group : group + 1, :], (SPAN, SPAN))
        rolled = pltpu.roll(spread, 0, 1, stride=1, stride_axis=0)
        toeplitz = jnp.where(causal, rolled, 0.0)
        high = toeplitz.astype(BF16)
        high_ref[0:SPAN, columns] = high
        low_ref[0:SPAN, columns] = (toeplitz - high.astype(F32)).astype(BF16)
        pick = (iota((GROUPS, SPAN), 0) == group).astype(F32)
        state = jnp.exp(-exact_dot(rates, pick, ((0,), (0,))) * left)
        high = state.astype(BF16)
        high_ref[SPAN : SPAN + ORDER, columns] = high
        low_ref[SPAN : SPAN + ORDER, columns] = (state - high.astype(F32)).astype(BF16)
    shape = (GROUPS, GROUPS * ORDER)
    mode_pick = iota((ORDER, shape[1]), 0) == iota((ORDER, shape[1]), 1) % ORDER
    own = iota(shape, 0) == iota(shape, 1) // ORDER

    def flat(values):
        wide = exact_dot(values, mode_pick.astype(F32), ((1,), (0,)))
        return jnp.sum(jnp.where(own, wide, 0.0), axis=0, keepdims=True)

    ahead = (iota((SPAN, shape[1]), 0) + 1).astype(F32)
    reach_ref[...] = flat(weights) * jnp.exp(-flat(rates) * ahead)
    lanes = iota((GROUPS, LANES), 1) % SIDE // FGROUP == iota((GROUPS, LANES), 0)
    decay_ref[...] = jnp.exp(-float(SPAN) * exact_dot(rates, lanes.astype(F32), ((0,), (0,))))


def deal_kernel(rows_ref, out_ref, edge_ref):
    rows = rows_ref[...].astype(F32)
    for pair in range(DEPTH // LANES):
        first = 2 * pair * LANES
        even = rows[:, first : first + LANES]
        odd = rows[:, first + LANES : first + 2 * LANES]
        columns = slice(pair * LANES, (pair + 1) * LANES)
        for core, value in enumerate(side_by_side(even, odd, 0)):
            value = value.astype(BF16)
            out_ref[core, :, columns] = value
            edge_ref[core, :, columns] = value[ROWS - HALO :]


def near_kernel(edge_ref, dealt_ref, out_ref):
    for run in range(2):
        out_ref[run, :, 0:HALO, :] = edge_ref[...]
        out_ref[run, :, HALO:, :] = dealt_ref[...]


def fan_kernel(near_ref, out_ref):
    for run in range(2):
        first, second = near_ref[run, 0], near_ref[run, 1, HALO:, :]
        for target in range(RING):
            out_ref[target, run, 0 : HALO + ROWS, :] = first
            out_ref[target, run, HALO + ROWS :, :] = second


LAST = (RING // 2, RING // 2 + 1)
FIRST = tuple(step for step in range(RING) if step not in LAST)


def add_products(x_ref, blocks, steps, totals):
    here = lax.axis_index("zh")
    core = lax.axis_index("core")
    for step, block in zip(steps, blocks):
        source = lax.rem(here + jnp.where(core == 0, RING - step, step), RING)
        slot = jnp.where(core == 0, source, RING - 1 - source)
        rows = [
            jnp.concatenate([block[near, part] for part in range(3)], axis=1)
            for near in range(4)
        ]
        weight = jnp.concatenate(rows, axis=0)
        totals = [
            total + jnp.dot(x_ref[slot, group], weight, preferred_element_type=F32)
            for group, total in enumerate(totals)
        ]
    return totals


def early_kernel(x_ref, *refs):
    totals = [jnp.zeros((HALO + SPAN, COLS), F32)] * 2
    refs[-1][0], refs[-1][1] = add_products(x_ref, refs[:-1], FIRST, totals)


def late_kernel(x_ref, sums_ref, *refs):
    blocks, (keep_ref, send_ref) = refs[: len(LAST)], refs[len(LAST) :]
    core = lax.axis_index("core")
    even, odd = add_products(x_ref, blocks, LAST, [sums_ref[0], sums_ref[1]])
    for part in range(3):
        columns = slice(part * LANES, (part + 1) * LANES)
        keep_ref[:, columns], send_ref[:, columns] = side_by_side(
            even[:, columns], odd[:, columns], core
        )


def scan_kernel(
    keep_ref, recv_ref, taps_ref, high_ref, low_ref, query_ref, signal_ref, local_ref, state_ref, rows_ref
):
    half, core = lax.axis_index("z0"), lax.axis_index("core")
    lanes = pl.ds(pl.multiple_of(half * LANES, LANES), LANES)
    total = keep_ref[...] + recv_ref[...]
    rows_ref[...] = total.astype(BF16).astype(F32)
    filtered = []
    for part in range(3):
        columns = slice(part * LANES, (part + 1) * LANES)
        taps = taps_ref[part, :, lanes]
        taps, _ = side_by_side(taps, taps, core)
        value = jnp.zeros((SPAN, LANES), F32)
        for tap in range(TAPS):
            value = value + taps[tap : tap + 1, :] * rows_ref[
                HALO - tap : HALO - tap + SPAN, columns
            ]
        filtered.append(value)
    query_ref[...] = filtered[0]
    signal = filtered[1] * filtered[2]
    signal_ref[...] = signal
    high = signal.astype(BF16)
    low = (signal - high.astype(F32)).astype(BF16)
    owner = iota((SPAN, LANES), 1) % SIDE // FGROUP
    acc = jnp.zeros((SPAN + ORDER, LANES), F32)
    for group in range(GROUPS):
        columns = slice(group * SPAN, (group + 1) * SPAN)
        mine = owner == group
        high_part = jnp.where(mine, high, jnp.zeros_like(high))
        low_part = jnp.where(mine, low, jnp.zeros_like(low))
        acc = acc + jnp.dot(high_ref[:, columns], high_part, preferred_element_type=F32)
        acc = acc + jnp.dot(high_ref[:, columns], low_part, preferred_element_type=F32)
        acc = acc + jnp.dot(low_ref[:, columns], high_part, preferred_element_type=F32)
    local_ref[...] = acc[0:SPAN]
    state_ref[...] = jnp.broadcast_to(
        acc[SPAN:][None], (PEERS, ORDER, LANES)
    )


def output_kernel(states_ref, decay_ref, reach_ref, query_ref, signal_ref, local_ref, gain_ref, out_ref):
    half, core = lax.axis_index("z0"), lax.axis_index("core")
    lanes = pl.ds(pl.multiple_of(half * LANES, LANES), LANES)
    low = iota((ORDER, LANES), 1) < SIDE
    place = 4 * lax.axis_index("zh") + lax.axis_index("yh") + jnp.where(low, 0, 2)
    decay = decay_ref[...]
    carry = jnp.zeros((ORDER, LANES), F32)
    for block in range(2 * PEERS - 1):
        outer, odd, yh = block // 4, block // 2 % 2, block % 2
        state = states_ref[outer * 2 + yh]
        other = pltpu.roll(state, SIDE, 1)
        state = jnp.where(low, other, state) if odd else jnp.where(low, state, other)
        carry = jnp.where(block < place, carry * decay + state, carry)
    tiled = jnp.concatenate([carry] * GROUPS, axis=0)
    shape = (GROUPS * ORDER, LANES)
    tiled = jnp.where(iota(shape, 0) // ORDER == iota(shape, 1) % SIDE // FGROUP, tiled, 0.0)
    conv = local_ref[...] + exact_dot(reach_ref[...], tiled, ((1,), (0,)))
    gain = jnp.broadcast_to(gain_ref[0:1, lanes], (8, LANES))
    gain, _ = side_by_side(gain, gain, core)
    mixed = query_ref[...] * (conv + gain[0:1] * signal_ref[...])
    for run, value in enumerate((mixed, pltpu.roll(mixed, SIDE, 1))):
        value = value[:, 0:SIDE].astype(BF16)
        for part in range(2):
            out_ref[run, part] = value[part * ROWS : (part + 1) * ROWS]


def call(kernel, shapes, *operands, scratch=(), limit=16):
    return pl.pallas_call(
        kernel,
        out_shape=[jax.ShapeDtypeStruct(shape, dtype) for shape, dtype in shapes],
        in_specs=[pl.BlockSpec(memory_space=pltpu.VMEM)] * len(operands),
        out_specs=[pl.BlockSpec(memory_space=pltpu.VMEM)] * len(shapes),
        scratch_shapes=list(scratch),
        compiler_params=pltpu.CompilerParams(vmem_limit_bytes=limit << 20),
    )(*operands)


def ring_shift(block, distance):
    route = []
    for i in range(RING):
        for core in range(2):
            target = (i + (distance if core == 0 else -distance)) % RING
            route.append((2 * i + core, 2 * target + core))
    return lax.ppermute(block, ("zh", "core"), route)


def per_device(sequence, in_weight, short_taps, decay_rates, residues, skip_gain):
    halves = [in_weight[:, :, side * LANES : (side + 1) * LANES] for side in range(2)]
    slots = jnp.stack([halves[0], halves[0], halves[1], halves[1]])
    block = lax.all_to_all(slots, ("z0", "yh"), 0, 0, tiled=True)
    blocks = [None] * RING
    blocks[0] = block
    up, down = block, block
    for step in range(1, RING // 2 + 1):
        up = ring_shift(up, 1)
        blocks[step] = up
        if step < RING // 2:
            down = ring_shift(down, -1)
            blocks[RING - step] = down
    count = 64
    dealt, edge = call(deal_kernel, [((2, ROWS, DEPTH), BF16), ((2, HALO, DEPTH), BF16)], sequence)
    edge = lax.ppermute(edge, CTX, [(i, i + 1) for i in range(count - 1)])
    (slots,) = call(near_kernel, [((2, 2, HALO + ROWS, DEPTH), BF16)], edge, dealt)
    near = lax.all_to_all(slots.reshape(4, HALO + ROWS, DEPTH), ("z0", "core"), 0, 0, tiled=True)
    (slots,) = call(
        fan_kernel, [((RING, 2, HALO + SPAN, DEPTH), BF16)], near.reshape(2, 2, HALO + ROWS, DEPTH)
    )
    peers = [list(range(RING)), list(range(2 * RING - 1, RING - 1, -1))]
    whole = lax.all_to_all(
        slots, ("core",) + CHAN, 0, 0, axis_index_groups=peers, tiled=True
    )

    high, low, reach, decay = call(
        filter_kernel,
        [
            ((SPAN + ORDER, GROUPS * SPAN), BF16),
            ((SPAN + ORDER, GROUPS * SPAN), BF16),
            ((SPAN, GROUPS * ORDER), F32),
            ((ORDER, LANES), F32),
        ],
        decay_rates,
        residues,
    )
    (sums,) = call(
        early_kernel, [((2, HALO + SPAN, COLS), F32)], whole, *[blocks[step] for step in FIRST]
    )
    keep, send = call(
        late_kernel, [((HALO + SPAN, COLS), F32)] * 2, whole, sums, *[blocks[step] for step in LAST]
    )
    recv = lax.ppermute(send, "core", [(0, 1), (1, 0)])
    query, signal, local, states = call(
        scan_kernel,
        [((SPAN, LANES), F32)] * 3 + [((PEERS, ORDER, LANES), F32)],
        keep,
        recv,
        short_taps,
        high,
        low,
        scratch=[pltpu.VMEM((HALO + SPAN, COLS), F32)],
    )
    states = lax.all_to_all(states, ("zh", "yh"), 0, 0, tiled=True)
    (slots,) = call(
        output_kernel,
        [((2, 2, ROWS, SIDE), BF16)],
        states,
        decay,
        reach,
        query,
        signal,
        local,
        skip_gain[None],
    )
    slots = lax.all_to_all(slots.reshape(4, ROWS, SIDE), ("z0", "core"), 0, 0, tiled=True)
    return slots.transpose(1, 0, 2).reshape(ROWS, 4 * SIDE)


def solution(mesh):
    fine = Mesh(mesh.devices.reshape(SIZES), AXES)
    return jax.shard_map(
        per_device,
        mesh=fine,
        in_specs=(
            P(CTX, CHAN),
            P(None, CTX, CHAN),
            P(None, None, CHAN),
            P(CHAN, None),
            P(CHAN, None),
            P(CHAN),
        ),
        out_specs=P(CTX, CHAN),
        check_vma=False,
    )
```
